32 devices in a mesh: groups: 2 (over x), dev: 8 (over z, y), rve: 2 (over core).
Axes of the slice: x: 2, y: 2, z: 4, core: 2. Of those that a mesh axis runs over, the one named last changes fastest.
Arguments:
- phase: int32 [4, 64, 128, 128], P(('groups', 'rve'), 'dev'), parts along dimension 0, may hold values from 0 to 2
- load_case: int32 [4], P(('groups', 'rve')), parts along dimension 0, may hold values from 0 to 5
- moduli: float32 [2, 3], replicated, may hold values from 0.5 to 8
- loading_table: float32 [6, 3, 3], replicated, may hold values from -4 to 4
- w_embed: bfloat16 [1408, 768], P(('dev', 'rve')), may hold values from -0.21875 to 0.21875
- w_up: bfloat16 [3072, 1408], P(('dev', 'rve')), may hold values from -0.15625 to 0.15625
- cotangent: bfloat16 [16384, 3072], P(('groups', 'dev', 'rve')), parts along dimension 0, may hold values from -6 to 6
Outputs:
- displacement: float32 [4, 3, 64, 128, 128], P(('groups', 'rve'), None, 'dev'), parts along dimension 0
- grad_embed: float32 [2816, 768], P(('groups', 'dev', 'rve')), parts along dimension 0
- grad_up: float32 [6144, 1408], P(('groups', 'dev', 'rve')), parts along dimension 0
The draws below stay inside these ranges and needn't reach their ends.
There are 2 independent parts, one for each index of `groups`. The reference program is written for one: setup_inputs(seed, part) draws one part's arguments, and reference() takes and returns one part's arrays. A program takes and returns all parts, laid end to end along the dimension named above; an argument that names none is the same for every part. Nothing has to cross between parts.
Inputs may be any that keep to these rules, and one draw needn't show every extreme that they name: `load_case`: row of loading_table for each RVE.
All inputs are finite; a program needn't handle non-finite values.
Results may differ from the reference program's by a relative error of at most 0.0069.
Values may be sent and summed in bfloat16 or wider, within the bound.
No kernel may reach another device: no remote copies, remote signals or barrier semaphores. Data moves between devices by JAX's collectives and lax.ppermute only.
A program may use at most 128 MiB of HBM per device.

```python
import math
from functools import partial
import jax
import jax.numpy as jnp
from jax import lax

D = 1408
FF = 3072
PATCH_X = 8
PATCH_Y = 8
PATCH_Z = 4
FEATURES = 768
NY = 128
NZ = 128
SWEEPS = 4
PHASES = 3
CASES = 6
NX = 64
RVES = 2
TOKENS = 8192
N_DEV = 8


def set_ends(array, stream_key, least, top_value):
    dims = array.shape
    place = [jax.random.randint(jax.random.fold_in(stream_key, axis), (), 0, dims[axis]) for axis in range(len(dims))]
    array = array.at[tuple(place)].set(least)
    longest = dims.index(max(dims))
    place[longest] = (place[longest] + 1) % dims[longest]
    return array.at[tuple(place)].set(top_value)


def strengthened(entries, key, source, target, shards_of, factor):
    owner, partner = [(jnp.arange(entries.shape[dim]) // (entries.shape[dim] // shards_of)).reshape([-1 if axis == dim else 1 for axis in range(entries.ndim)]) for dim in (source, target)]
    chosen = jax.random.permutation(key, shards_of)[partner]
    strong = (owner == chosen) | (owner == (partner + shards_of // 2) % shards_of)
    return jnp.where(strong, factor * entries, entries)


def steps_of(own_key, shape, cuts, least, largest):
    def one(position, parts):
        draws = jax.random.uniform(jax.random.fold_in(jax.random.fold_in(own_key, 6), position), (parts,), jnp.float32, least / len(cuts), largest / len(cuts))
        return jnp.repeat(jnp.exp(draws), shape[position] // parts).reshape((-1,) + (1,) * (len(shape) - position - 1))

    factor_of = one(*cuts[0])
    for cut in cuts[1:]:
        factor_of = factor_of * one(*cut)
    return factor_of


def centred(rng, extent, deviation, bound, pieces=(), kind=jnp.bfloat16):
    result = jax.random.normal(rng, extent, jnp.float32) * deviation
    if len(pieces) > 0:
        result = steps_of(rng, extent, pieces, -0.22, 0.18) * result
    return jnp.clip(result, min=-bound, max=bound).astype(kind)


def noise_with(key, extent, spread, reach, split, heavy, kind=jnp.bfloat16):
    values = spread * jax.random.normal(key, extent, jnp.float32)
    if split:
        values = values * steps_of(key, extent, split, -0.22, 0.18)
    return jnp.clip(strengthened(values, jax.random.fold_in(key, 3), *heavy), -reach, reach).astype(kind)


def setup_inputs(seed: int = 0, part: int = 0) -> dict:
    key_of = jax.random.split(jax.random.key(seed), 8)
    part_splits = jax.random.split(jax.random.fold_in(key_of[7], part), 8)
    return {
        "phase": set_ends(jax.random.randint(part_splits[0], (RVES, NX, NY, NZ), 0, PHASES), jax.random.fold_in(part_splits[0], 1), 0, PHASES - 1).astype(jnp.int32),
        "load_case": jax.random.randint(part_splits[1], (RVES,), 0, CASES).astype(jnp.int32),
        "moduli": jnp.clip(jnp.exp(jax.random.uniform(key_of[2], (2, PHASES), jnp.float32, math.log(0.5), math.log(8.0))), 0.5, 8.0),
        "loading_table": centred(key_of[3], (CASES, 3, 3), 1.0, 4.0, (), jnp.float32),
        "w_embed": centred(key_of[4], (D, FEATURES), FEATURES ** -0.5, 0.21875, ((0, 16),)),
        "w_up": centred(key_of[5], (FF, D), D ** -0.5, 0.15625, ((0, 16),)),
        "cotangent": noise_with(part_splits[6], (TOKENS, FF), 1.0, 6.0, ((0, 16),), (0, 1, 16, 2.0)),
    }


epsilon = 1e-06

def stiffness(phase, moduli):
    labels = jnp.arange(moduli.shape[1], dtype=jnp.int32)
    member = (labels[:, None, None, None] == phase[None]).astype(jnp.float32)
    shear_stiff = lax.optimization_barrier(jnp.sum(member * moduli[0][:, None, None, None], axis=0))
    axial_stiff = lax.optimization_barrier(jnp.sum(member * moduli[1][:, None, None, None], axis=0))
    return (shear_stiff, axial_stiff)

def harmonic(here, there, in_here, in_there):
    blended = 2.0 * here * there / (here + there)
    return jnp.where(in_here & in_there, blended, jnp.where(in_here, here, there))

def face_pairs(stiff, inside):
    stiff = jnp.where(inside, stiff, 1.0)
    padded = jnp.pad(stiff, 1, constant_values=1.0)
    in_pad = jnp.pad(inside, 1)
    face_list = []
    for direction in range(3):
        upper_cut = [slice(1, -1)] * 3
        lower_cut = [slice(1, -1)] * 3
        upper_cut[direction] = slice(2, None)
        lower_cut[direction] = slice(0, -2)
        upper_face = harmonic(stiff, padded[tuple(upper_cut)], inside, in_pad[tuple(upper_cut)])
        lower_face = harmonic(stiff, padded[tuple(lower_cut)], inside, in_pad[tuple(lower_cut)])
        face_list.append((upper_face, lower_face))
    return face_list

def operator_terms(shear_stiff, axial_stiff, inside, strain):
    shear_faces = face_pairs(shear_stiff, inside)
    axial_faces = face_pairs(axial_stiff, inside)
    terms = []
    for component in range(3):
        face_list = [axial_faces[direction] if direction == component else shear_faces[direction] for direction in range(3)]
        forcing = strain[component, 0] * (face_list[0][0] - face_list[0][1])
        diagonal = face_list[0][0] + face_list[0][1]
        for direction in (1, 2):
            forcing = forcing + strain[component, direction] * (face_list[direction][0] - face_list[direction][1])
            diagonal = diagonal + face_list[direction][0] + face_list[direction][1]
        terms.append((face_list, forcing, diagonal))
    return terms

def first_iterate(terms, inside):
    return jnp.stack([jnp.where(inside, forcing / diagonal, 0.0) for face_list, forcing, diagonal in terms])

def jacobi_sweep(ghosted, terms, inside):
    results = []
    for component in range(3):
        face_list, forcing, diagonal = terms[component]
        padded = jnp.pad(ghosted[component], ((0, 0), (1, 1), (1, 1)))
        summed = forcing
        for direction in range(3):
            upper_cut = [slice(1, -1)] * 3
            lower_cut = [slice(1, -1)] * 3
            upper_cut[direction] = slice(2, None)
            lower_cut[direction] = slice(0, -2)
            summed = summed + face_list[direction][0] * padded[tuple(upper_cut)] + face_list[direction][1] * padded[tuple(lower_cut)]
        results.append(jnp.where(inside, summed / diagonal, 0.0))
    return jnp.stack(results)

def gelu_grad(pre_act, cotangent):
    _, pullback = jax.vjp(partial(jax.nn.gelu, approximate=True), pre_act)
    return pullback(cotangent.astype(jnp.float32))[0].astype(jnp.bfloat16)

def reference(phase, load_case, moduli, loading_table, w_embed, w_up, cotangent):
    fields = []
    for member_index in range(RVES):
        shear_stiff, axial_stiff = stiffness(phase[member_index], moduli)
        strain = loading_table[load_case[member_index]]
        inside = jnp.ones(phase.shape[1:], dtype=bool)
        terms = operator_terms(shear_stiff, axial_stiff, inside, strain)
        displace = first_iterate(terms, inside)
        for repeat in range(SWEEPS - 1):
            displace = jacobi_sweep(jnp.pad(displace, ((0, 0), (1, 1), (0, 0), (0, 0))), terms, inside)
        fields.append(displace)
    displacement = jnp.stack(fields)
    cells = displacement.astype(jnp.bfloat16).reshape(RVES, 3, NX // PATCH_X, PATCH_X, N_DEV, NY // (N_DEV * PATCH_Y), PATCH_Y, NZ // PATCH_Z, PATCH_Z)
    patches = cells.transpose(4, 0, 5, 2, 7, 1, 3, 6, 8).reshape(TOKENS, FEATURES)
    grad_scale = 1.0 / math.sqrt(TOKENS)
    embedded = jnp.dot(patches, w_embed.T, preferred_element_type=jnp.float32).astype(jnp.bfloat16)
    embed_wide = embedded.astype(jnp.float32)
    inverse_rms = lax.rsqrt(lax.optimization_barrier(jnp.mean(embed_wide * embed_wide, axis=-1, keepdims=True)) + epsilon)
    normed_wide = embed_wide * inverse_rms
    normed = normed_wide.astype(jnp.bfloat16)
    pre_act = jnp.dot(normed, w_up.T, preferred_element_type=jnp.float32)
    act_grad = gelu_grad(pre_act, cotangent)
    grad_up = jnp.dot(act_grad.T, normed, preferred_element_type=jnp.float32) * grad_scale
    normed_grad = jnp.dot(act_grad, w_up, preferred_element_type=jnp.float32)
    embed_in_grad = (inverse_rms * (normed_grad - normed_wide * lax.optimization_barrier(jnp.mean(normed_grad * normed_wide, axis=-1, keepdims=True)))).astype(jnp.bfloat16)
    grad_embed = jnp.dot(embed_in_grad.T, patches, preferred_element_type=jnp.float32) * grad_scale
    return (displacement, grad_embed, grad_up)
```

```python
from functools import partial
import math

import jax
import jax.numpy as jnp
from jax import lax
from jax.experimental import pallas as pl
from jax.experimental.pallas import tpu as pltpu
from jax.sharding import PartitionSpec as P

PATCH_X = 8
PATCH_Y = 8
PATCH_Z = 4
SWEEPS = 4


epsilon = 1e-06
bf16 = jnp.bfloat16
f32 = jnp.float32
VMEM_LIMIT = 60 * 1024 * 1024


def contract(left, right, left_dim, right_dim):
    return lax.dot_general(
        left, right, (((left_dim,), (right_dim,)), ((), ())), preferred_element_type=f32
    )


def exchange(value, axis, bit):
    size = lax.axis_size(axis)
    return lax.ppermute(value, axis, [(i, i ^ bit) for i in range(size)])


def shifted(plane, axis, step):
    return pltpu.roll(plane, step % plane.shape[axis], axis)


def solver_kernel(
    scalars, tables, loading, phase_ref, before_ref, after_ref, displace_ref, *rest, slab, bands, patch_y
):
    block_refs = rest[:bands]
    key, face, self_x, rdiag, force, even, odd = rest[bands:]
    halo = SWEEPS
    total = slab + 2 * halo
    phases = tables.shape[1]
    me, first_row, grid_rows, case = (scalars[i] for i in range(4))
    ny, nz = phase_ref.shape[1:]
    iota_y = lax.broadcasted_iota(jnp.int32, (ny, nz), 0)
    iota_z = lax.broadcasted_iota(jnp.int32, (ny, nz), 1)
    pairs = [(p, q) for p in range(phases) for q in range(p, phases)]

    def power(labels):
        result = jnp.full(labels.shape, 1, jnp.int32)
        for p in range(1, phases):
            result = jnp.where(labels == p, 1 << p, result)
        return result

    key[pl.ds(halo, slab)] = power(phase_ref[...])
    key[pl.ds(0, halo)] = power(before_ref[...].astype(f32).astype(jnp.int32))
    key[pl.ds(halo + slab, halo)] = power(after_ref[...].astype(f32).astype(jnp.int32))

    @pl.when(first_row == 0)
    def _():
        key[halo - 1] = key[halo]

    @pl.when(first_row + slab == grid_rows)
    def _():
        key[halo + slab] = key[halo + slab - 1]

    def faces(here, there):
        code = here + there
        results = [jnp.full(code.shape, tables[kind, 0, 0], f32) for kind in range(2)]
        for p, q in pairs[1:]:
            hit = code == ((1 << p) + (1 << q))
            for kind in range(2):
                results[kind] = jnp.where(hit, tables[kind, p, q], results[kind])
        return results

    def x_faces(row, carry):
        for kind, value in enumerate(faces(key[row], key[row + 1])):
            self_x[kind, row] = value
        return carry

    lax.fori_loop(0, total - 1, x_faces, 0)

    strain = [[loading[case, 3 * c + a] for a in range(3)] for c in range(3)]

    def setup(row, carry):
        here = key[row]
        own = faces(here, here)
        above_y = jnp.where(iota_y == ny - 1, here, shifted(here, 0, -1))
        above_z = jnp.where(iota_z == nz - 1, here, shifted(here, 1, -1))
        upper_y = faces(here, above_y)
        upper_z = faces(here, above_z)
        gaps, sums = ([], [])
        for kind in range(2):
            face[kind, 0, row] = jnp.where(iota_y == ny - 1, 0.0, upper_y[kind])
            face[kind, 1, row] = jnp.where(iota_z == nz - 1, 0.0, upper_z[kind])
            lower_y = jnp.where(iota_y == 0, own[kind], shifted(upper_y[kind], 0, 1))
            lower_z = jnp.where(iota_z == 0, own[kind], shifted(upper_z[kind], 1, 1))
            upper_x, lower_x = (self_x[kind, row], self_x[kind, row - 1])
            gaps.append([upper_x - lower_x, upper_y[kind] - lower_y, upper_z[kind] - lower_z])
            sums.append([upper_x + lower_x, upper_y[kind] + lower_y, upper_z[kind] + lower_z])
        global_row = first_row + row - halo
        inside = jnp.where((global_row >= 0) & (global_row < grid_rows), 1.0, 0.0)
        for c in range(3):
            kinds = [1 if a == c else 0 for a in range(3)]
            forcing = sum(strain[c][a] * gaps[kinds[a]][a] for a in range(3))
            diagonal = sums[kinds[0]][0] + sums[kinds[1]][1] + sums[kinds[2]][2]
            inverse = inside / diagonal
            rdiag[c, row] = inverse
            force[c, row] = forcing
            even[c, row] = forcing * inverse
        return carry

    lax.fori_loop(1, total - 1, setup, 0)

    buffers = (even, odd)
    for step in range(1, SWEEPS):
        source, target = (buffers[(step - 1) % 2], buffers[step % 2])

        def sweep(row, carry, source=source, target=target, last=step == SWEEPS - 1):
            for c in range(3):
                kx, ky, kz = (1 if a == c else 0 for a in range(3))
                here = source[c, row]
                face_y = face[ky, 0, row]
                face_z = face[kz, 1, row]
                summed = (
                    force[c, row]
                    + self_x[kx, row] * source[c, row + 1]
                    + self_x[kx, row - 1] * source[c, row - 1]
                    + face_y * shifted(here, 0, -1)
                    + shifted(face_y * here, 0, 1)
                    + face_z * shifted(here, 1, -1)
                    + shifted(face_z * here, 1, 1)
                )
                value = summed * rdiag[c, row]
                target[c, row] = value
                if last:
                    displace_ref[c, row - halo] = value
            return carry

        lax.fori_loop(1 + step, total - 1 - step, sweep, 0)

    band_rows = ny // bands
    for k in range(bands):
        band = me ^ k
        at = 0
        for b in range(band_rows // patch_y):
            start = pl.multiple_of(band * band_rows + b * patch_y, patch_y)
            for c in range(3):
                for x in range(0, slab, 2):
                    pair = jnp.concatenate(
                        [displace_ref[c, x + i, pl.ds(start, patch_y), :] for i in range(2)], axis=0
                    )
                    block_refs[k][pl.ds(at, 2 * patch_y), :] = pair.astype(bf16)
                    at += 2 * patch_y


def solve(phase, before, after, scalars, tables, loading, bands):
    slab, ny, nz = phase.shape
    total = slab + 2 * SWEEPS
    rows = 3 * slab * ny // bands
    smem = pl.BlockSpec(memory_space=pltpu.SMEM)
    vmem = pl.BlockSpec(memory_space=pltpu.VMEM)
    plane = (ny, nz)
    return pl.pallas_call(
        partial(solver_kernel, slab=slab, bands=bands, patch_y=PATCH_Y),
        out_shape=[jax.ShapeDtypeStruct((3, slab) + plane, f32)]
        + [jax.ShapeDtypeStruct((rows, nz), bf16)] * bands,
        in_specs=[smem, smem, smem, vmem, vmem, vmem],
        out_specs=[vmem] * (1 + bands),
        scratch_shapes=[
            pltpu.VMEM((total,) + plane, jnp.int32),
            pltpu.VMEM((2, 2, total) + plane, f32),
            pltpu.VMEM((2, total) + plane, f32),
            pltpu.VMEM((3, total) + plane, f32),
            pltpu.VMEM((3, total) + plane, f32),
            pltpu.VMEM((3, total) + plane, f32),
            pltpu.VMEM((3, total) + plane, f32),
        ],
        compiler_params=pltpu.CompilerParams(vmem_limit_bytes=VMEM_LIMIT),
        cost_estimate=pl.CostEstimate(flops=40_000_000, bytes_accessed=4_000_000, transcendentals=0),
        name="solver",
    )(scalars, tables, loading, phase, before, after)


def patch_kernel(scalars, *refs, slabs, bands_in):
    block_refs, (perm_ref, order_ref, out_ref, plain_ref, held) = (refs[:slabs], refs[slabs:])
    rows, lanes = block_refs[0].shape
    rows = rows // bands_in
    me = scalars[0]
    for k in range(slabs):
        held[k] = block_refs[k][...]
    group = PATCH_Z
    for g in range(slabs * bands_in // group):
        parts = []
        for j in range(group):
            b, px = divmod(group * g + j, slabs)
            parts.append(held[me ^ px, pl.ds(b * rows, rows), :])
        moved = jnp.dot(
            jnp.concatenate(parts, axis=1), perm_ref[...], preferred_element_type=f32
        ).astype(bf16)
        for z in range(group):
            out_ref[pl.ds(z * rows, rows), pl.ds(g * lanes, lanes)] = moved[:, z * lanes : (z + 1) * lanes]
    plain_ref[...] = jnp.dot(order_ref[...], out_ref[...], preferred_element_type=f32).astype(bf16)


def patchify(blocks, scalars, bands_in):
    slabs = len(blocks)
    rows, nz = blocks[0].shape
    rows = rows // bands_in
    cells = nz // PATCH_Z
    width = PATCH_Z * nz
    features = PATCH_Z * rows
    tokens = slabs * bands_in * cells
    lane = jnp.arange(width, dtype=jnp.int32)
    j, pz, z = (lane // nz, lane % nz // PATCH_Z, lane % PATCH_Z)
    perm = ((z * nz + j * cells + pz)[:, None] == lane[None]).astype(bf16)
    feature = jnp.arange(features, dtype=jnp.int32)
    order = (((feature % PATCH_Z) * rows + feature // PATCH_Z)[:, None] == feature[None]).astype(bf16)
    vmem = pl.BlockSpec(memory_space=pltpu.VMEM)
    return pl.pallas_call(
        partial(patch_kernel, slabs=slabs, bands_in=bands_in),
        out_shape=[jax.ShapeDtypeStruct((features, tokens), bf16)] * 2,
        in_specs=[pl.BlockSpec(memory_space=pltpu.SMEM)] + [vmem] * (slabs + 2),
        out_specs=[vmem] * 2,
        scratch_shapes=[pltpu.VMEM((slabs, rows * bands_in, nz), bf16)],
        compiler_params=pltpu.CompilerParams(vmem_limit_bytes=VMEM_LIMIT),
        cost_estimate=pl.CostEstimate(flops=1_000_000_000, bytes_accessed=5_000_000, transcendentals=0),
        name="patchify",
    )(scalars, *blocks, perm, order)


def turn_kernel(scalars, cot_ref, own_ref, other_ref, held):
    per, hidden = own_ref.shape[:2]
    held[...] = cot_ref[...].T
    me, core = (scalars[0], scalars[1])
    for i in range(per):
        slot = (me % per) ^ i
        start = 2 * i * hidden
        own_ref[slot] = held[pl.ds(pl.multiple_of(start + core * hidden, hidden), hidden), :]
        other_ref[slot] = held[pl.ds(pl.multiple_of(start + (1 - core) * hidden, hidden), hidden), :]


def turn(cotangent, scalars, blocks):
    tokens, hidden = cotangent.shape
    width = hidden // blocks
    per = 1
    while per * width % 128:
        per *= 2
    out = jax.ShapeDtypeStruct((blocks, width // 2, tokens), bf16)
    out_spec = pl.BlockSpec((per, width // 2, tokens), lambda i, s: ((s[0] // per) ^ i, 0, 0))
    return pl.pallas_call(
        turn_kernel,
        out_shape=[out, out],
        grid_spec=pltpu.PrefetchScalarGridSpec(
            num_scalar_prefetch=1,
            grid=(blocks // per,),
            in_specs=[pl.BlockSpec((tokens, per * width), lambda i, s: (0, i))],
            out_specs=[out_spec, out_spec],
            scratch_shapes=[pltpu.VMEM((per * width, tokens), bf16)],
        ),
        cost_estimate=pl.CostEstimate(flops=0, bytes_accessed=6_300_000, transcendentals=0),
        name="turn",
    )(scalars, cotangent)


def gather_slots(shard, axis):
    size = lax.axis_size(axis)
    slots = [None] * size
    slots[0] = shard
    bits = [1 << i for i in range(size.bit_length() - 1)]
    known = [0]
    for bit in bits[:0:-1]:
        for k in list(known):
            slots[k ^ bit] = exchange(slots[k], axis, bit)
            known.append(k ^ bit)
    for k in list(known):
        slots[k ^ 1] = exchange(slots[k], axis, 1)
    return slots


def scatter_slots(slots, axis):
    size = lax.axis_size(axis)
    bits = [1 << i for i in range(size.bit_length() - 1)]
    live = dict(enumerate(slots))
    for bit in bits:
        for k in sorted(k for k in live if k & bit):
            arrived = exchange(live.pop(k), axis, bit)
            total = live[k ^ bit].astype(f32) + arrived.astype(f32)
            live[k ^ bit] = total if bit == bits[-1] else total.astype(bf16)
    return live[0]


def gelu_grad(pre_act, cotangent):
    _, pullback = jax.vjp(partial(jax.nn.gelu, approximate=True), pre_act)
    return pullback(cotangent.astype(f32))[0].astype(bf16)


def swap(value):
    return exchange(value, "rve", 1)


def local(phase, load_case, moduli, loading_table, w_embed, w_up, cotangent):
    phase = phase[0]
    slab, ny, nz = phase.shape
    devs = lax.axis_size("dev")
    me = lax.axis_index("dev")
    core = lax.axis_index("rve")
    features = w_embed.shape[1]
    rows_embed = w_embed.shape[0]
    hidden = w_up.shape[0]
    tokens = cotangent.shape[0]
    bands_in = ny // devs // PATCH_Y
    grad_scale = 1.0 / math.sqrt(tokens * devs * 2)

    small = phase.astype(bf16)
    up = [(i, i + 1) for i in range(devs - 1)]
    down = [(j, i) for i, j in up]
    before = lax.ppermute(small[slab - SWEEPS :], "dev", up)
    after = lax.ppermute(small[:SWEEPS], "dev", down)

    blend = 2.0 * moduli[:, :, None] * moduli[:, None, :] / (moduli[:, :, None] + moduli[:, None, :])
    count = moduli.shape[1]
    tables = jnp.where(jnp.eye(count, dtype=bool)[None], moduli[:, :, None], blend)
    scalars = jnp.stack([me * 1, me * slab, slab * devs + 0 * me, load_case[0]]).astype(jnp.int32)
    places = jnp.stack([me, core]).astype(jnp.int32)
    outs = solve(phase, before, after, scalars, tables, loading_table.reshape(loading_table.shape[0], 9), devs)
    displace, blocks = (outs[0], outs[1:])

    feature = jnp.arange(features, dtype=jnp.int32)
    order = (((feature % PATCH_Z) * (features // PATCH_Z) + feature // PATCH_Z)[:, None] == feature[None]).astype(bf16)
    embed_rows = jnp.dot(w_embed, order, preferred_element_type=f32).astype(bf16)
    embed_slots = jnp.stack(gather_slots(embed_rows, "dev"))
    embed_other = swap(embed_slots)
    first = jnp.where(core == 0, embed_slots, embed_other)
    second = jnp.where(core == 0, embed_other, embed_slots)
    both = jnp.stack([first, second], axis=1)
    both = jnp.take(both, me ^ jnp.arange(devs, dtype=jnp.int32), axis=0)
    w_all = both.reshape(devs * 2 * rows_embed, features)

    up_slots = gather_slots(w_up, "dev")
    up_all = jnp.concatenate(up_slots, axis=0)

    cot_own, cot_other = turn(cotangent, places, devs)
    cot_arrived = swap(cot_other)
    cot = jnp.concatenate([cot_own, cot_arrived], axis=2).reshape(devs * hidden, 2 * tokens)

    arrived = [blocks[0]] + [exchange(blocks[k], "dev", k) for k in range(1, devs)]
    patches, plain = patchify(arrived, places, bands_in)
    patches_both = jnp.concatenate([patches, swap(patches)], axis=1)

    embedded = contract(w_all, patches_both, 1, 0).astype(bf16)
    embed_wide = embedded.astype(f32)
    inverse_rms = lax.rsqrt(jnp.mean(embed_wide * embed_wide, axis=0, keepdims=True) + epsilon)
    normed = (embed_wide * inverse_rms).astype(bf16)

    half = devs // 2
    cut = half * hidden
    act_parts, grad_parts = ([], [])
    for part in range(2):
        rows = slice(part * cut, (part + 1) * cut)
        pre_act = contract(up_all[rows], normed, 1, 0)
        act = gelu_grad(pre_act, cot[rows])
        act_parts.append(act)
        grad_parts.append(contract(act, normed, 1, 1).astype(bf16))
    grads = [
        grad_parts[k // half][(k % half) * hidden : (k % half + 1) * hidden] for k in range(devs)
    ]
    grad_up = scatter_slots(grads, "dev") * grad_scale

    act_all = jnp.concatenate(act_parts, axis=0)
    normed_grad = contract(up_all, act_all, 0, 0)
    partner = swap(normed_grad[:, tokens:].astype(bf16))
    total_grad = normed_grad[:, :tokens] + partner.astype(f32)
    own_wide = embed_wide[:, :tokens] * inverse_rms[:, :tokens]
    inner = jnp.mean(total_grad * own_wide, axis=0, keepdims=True)
    embed_in = (inverse_rms[:, :tokens] * (total_grad - own_wide * inner)).astype(bf16)
    grad_all = contract(embed_in, plain, 1, 1).astype(bf16).reshape(devs, 2, rows_embed, features)
    grad_all = jnp.take(grad_all, me ^ jnp.arange(devs, dtype=jnp.int32), axis=0)
    mine = jnp.where(core == 0, grad_all[:, 0], grad_all[:, 1])
    yours = jnp.where(core == 0, grad_all[:, 1], grad_all[:, 0])
    mine = (mine.astype(f32) + swap(yours).astype(f32)).astype(bf16)
    grad_embed = scatter_slots([mine[k] for k in range(devs)], "dev") * grad_scale
    return (displace[None], grad_embed, grad_up)


def solution(mesh):
    return jax.shard_map(
        local,
        mesh=mesh,
        in_specs=(
            P(("groups", "rve"), "dev", None, None),
            P(("groups", "rve")),
            P(),
            P(),
            P(("dev", "rve"), None),
            P(("dev", "rve"), None),
            P(("groups", "dev", "rve"), None),
        ),
        out_specs=(
            P(("groups", "rve"), None, "dev", None, None),
            P(("groups", "dev", "rve"), None),
            P(("groups", "dev", "rve"), None),
        ),
        check_vma=False,
    )
```

```python
from functools import partial
import math

import jax
import jax.numpy as jnp
from jax import lax
from jax.experimental import pallas as pl
from jax.experimental.pallas import tpu as pltpu
from jax.sharding import PartitionSpec as P


PATCH_Y = 8
PATCH_Z = 4
SWEEPS = 4


epsilon = 1e-06
bf16 = jnp.bfloat16
f32 = jnp.float32
MIB = 1024 * 1024


def contract(left, right, left_dim, right_dim):
    return lax.dot_general(
        left, right, (((left_dim,), (right_dim,)), ((), ())), preferred_element_type=f32
    )


def exchange(value, axis, bit):
    size = lax.axis_size(axis)
    return lax.ppermute(value, axis, [(i, i ^ bit) for i in range(size)])


def shifted(plane, axis, step):
    return pltpu.roll(plane, step % plane.shape[axis], axis)


def solver_kernel(
    scalars, tables, loading, phase_ref, before_ref, after_ref, displace_ref, *rest, slab, bands, patch_y
):
    block_refs = rest[:bands]
    key, face, self_x, rdiag, force, even, odd = rest[bands:]
    halo = SWEEPS
    total = slab + 2 * halo
    phases = tables.shape[1]
    me, case = (scalars[0], scalars[2])
    first_row, grid_rows = (me * slab, slab * bands)
    ny, nz = phase_ref.shape[1:]
    iota_y = lax.broadcasted_iota(jnp.int32, (ny, nz), 0)
    iota_z = lax.broadcasted_iota(jnp.int32, (ny, nz), 1)
    pairs = [(p, q) for p in range(phases) for q in range(p, phases)]

    def blend(kind, p, q):
        here, there = (jnp.full((1, nz), tables[kind, i], f32) for i in (p, q))
        return here if p == q else 2.0 * here * there / (here + there)

    values = {(kind, p, q): blend(kind, p, q) for p, q in pairs for kind in range(2)}

    def power(labels):
        result = jnp.full(labels.shape, 1, jnp.int32)
        for p in range(1, phases):
            result = jnp.where(labels == p, 1 << p, result)
        return result

    key[pl.ds(halo, slab)] = power(phase_ref[...])
    key[pl.ds(0, halo)] = power(before_ref[...].astype(f32).astype(jnp.int32))
    key[pl.ds(halo + slab, halo)] = power(after_ref[...].astype(f32).astype(jnp.int32))

    @pl.when(first_row == 0)
    def _():
        key[halo - 1] = key[halo]

    @pl.when(first_row + slab == grid_rows)
    def _():
        key[halo + slab] = key[halo + slab - 1]

    def faces(here, there):
        code = here + there
        results = [jnp.broadcast_to(values[kind, 0, 0], code.shape) for kind in range(2)]
        for p, q in pairs[1:]:
            hit = code == ((1 << p) + (1 << q))
            for kind in range(2):
                results[kind] = jnp.where(hit, values[kind, p, q], results[kind])
        return results

    def x_faces(row, carry):
        for kind, value in enumerate(faces(key[row], key[row + 1])):
            self_x[kind, row] = value
        return carry

    lax.fori_loop(0, total - 1, x_faces, 0)

    strain = [[loading[case, c, a] for a in range(3)] for c in range(3)]

    def setup(row, carry):
        here = key[row]
        own = faces(here, here)
        above_y = jnp.where(iota_y == ny - 1, here, shifted(here, 0, -1))
        above_z = jnp.where(iota_z == nz - 1, here, shifted(here, 1, -1))
        upper_y = faces(here, above_y)
        upper_z = faces(here, above_z)
        gaps, sums = ([], [])
        for kind in range(2):
            face[kind, 0, row] = jnp.where(iota_y == ny - 1, 0.0, upper_y[kind])
            face[kind, 1, row] = jnp.where(iota_z == nz - 1, 0.0, upper_z[kind])
            lower_y = jnp.where(iota_y == 0, own[kind], shifted(upper_y[kind], 0, 1))
            lower_z = jnp.where(iota_z == 0, own[kind], shifted(upper_z[kind], 1, 1))
            upper_x, lower_x = (self_x[kind, row], self_x[kind, row - 1])
            gaps.append([upper_x - lower_x, upper_y[kind] - lower_y, upper_z[kind] - lower_z])
            sums.append([upper_x + lower_x, upper_y[kind] + lower_y, upper_z[kind] + lower_z])
        global_row = first_row + row - halo
        inside = jnp.where((global_row >= 0) & (global_row < grid_rows), 1.0, 0.0)
        for c in range(3):
            kinds = [1 if a == c else 0 for a in range(3)]
            forcing = sum(strain[c][a] * gaps[kinds[a]][a] for a in range(3))
            diagonal = sums[kinds[0]][0] + sums[kinds[1]][1] + sums[kinds[2]][2]
            inverse = inside / diagonal
            rdiag[c, row] = inverse
            force[c, row] = forcing
            even[c, row] = forcing * inverse
        return carry

    lax.fori_loop(1, total - 1, setup, 0)

    buffers = (even, odd)
    for step in range(1, SWEEPS):
        source, target = (buffers[(step - 1) % 2], buffers[step % 2])

        def sweep(row, carry, source=source, target=target, last=step == SWEEPS - 1):
            for c in range(3):
                kx, ky, kz = (1 if a == c else 0 for a in range(3))
                here = source[c, row]
                face_y = face[ky, 0, row]
                face_z = face[kz, 1, row]
                summed = (
                    force[c, row]
                    + self_x[kx, row] * source[c, row + 1]
                    + self_x[kx, row - 1] * source[c, row - 1]
                    + face_y * shifted(here, 0, -1)
                    + shifted(face_y * here, 0, 1)
                    + face_z * shifted(here, 1, -1)
                    + shifted(face_z * here, 1, 1)
                )
                value = summed * rdiag[c, row]
                target[c, row] = value
                if last:
                    displace_ref[c, row - halo] = value
            return carry

        lax.fori_loop(1 + step, total - 1 - step, sweep, 0)

    band_rows = ny // bands
    for k in range(bands):
        band = me ^ k
        at = 0
        for b in range(band_rows // patch_y):
            start = pl.multiple_of(band * band_rows + b * patch_y, patch_y)
            for c in range(3):
                for x in range(0, slab, 2):
                    pair = jnp.concatenate(
                        [displace_ref[c, x + i, pl.ds(start, patch_y), :] for i in range(2)], axis=0
                    )
                    block_refs[k][pl.ds(at, 2 * patch_y), :] = pair.astype(bf16)
                    at += 2 * patch_y


def solve(phase, before, after, scalars, tables, loading, bands):
    slab, ny, nz = phase.shape
    total = slab + 2 * SWEEPS
    rows = 3 * slab * ny // bands
    smem = pl.BlockSpec(memory_space=pltpu.SMEM)
    vmem = pl.BlockSpec(memory_space=pltpu.VMEM)
    plane = (ny, nz)
    return pl.pallas_call(
        partial(solver_kernel, slab=slab, bands=bands, patch_y=PATCH_Y),
        out_shape=[jax.ShapeDtypeStruct((3, slab) + plane, f32)]
        + [jax.ShapeDtypeStruct((rows, nz), bf16)] * bands,
        in_specs=[smem, smem, smem, vmem, vmem, vmem],
        out_specs=[vmem] * (1 + bands),
        scratch_shapes=[
            pltpu.VMEM((total,) + plane, jnp.int32),
            pltpu.VMEM((2, 2, total) + plane, f32),
            pltpu.VMEM((2, total) + plane, f32),
            pltpu.VMEM((3, total) + plane, f32),
            pltpu.VMEM((3, total) + plane, f32),
            pltpu.VMEM((3, total) + plane, f32),
            pltpu.VMEM((3, total) + plane, f32),
        ],
        compiler_params=pltpu.CompilerParams(vmem_limit_bytes=30 * MIB),
        cost_estimate=pl.CostEstimate(flops=40_000_000, bytes_accessed=4_000_000, transcendentals=0),
        name="solver",
    )(scalars, tables, loading, phase, before, after)


def feature_order(features):
    feature = jnp.arange(features, dtype=jnp.int32)
    source = (feature % PATCH_Z) * (features // PATCH_Z) + feature // PATCH_Z
    return (feature[:, None] == source[None]).astype(bf16)


def patch_kernel(scalars, *refs, slabs, bands_in):
    block_refs, (perm_ref, order_ref, out_ref, plain_ref, held) = (refs[:slabs], refs[slabs:])
    rows, lanes = block_refs[0].shape
    rows = rows // bands_in
    me = scalars[0]
    for k in range(slabs):
        held[k] = block_refs[k][...]
    group = PATCH_Z
    for g in range(slabs * bands_in // group):
        parts = []
        for j in range(group):
            b, px = divmod(group * g + j, slabs)
            parts.append(held[me ^ px, pl.ds(b * rows, rows), :])
        moved = jnp.dot(
            jnp.concatenate(parts, axis=1), perm_ref[...], preferred_element_type=f32
        ).astype(bf16)
        for z in range(group):
            out_ref[pl.ds(z * rows, rows), pl.ds(g * lanes, lanes)] = moved[:, z * lanes : (z + 1) * lanes]
    plain_ref[...] = jnp.dot(order_ref[...], out_ref[...], preferred_element_type=f32).astype(bf16)


def patchify(blocks, scalars, bands_in):
    slabs = len(blocks)
    rows, nz = blocks[0].shape
    rows = rows // bands_in
    cells = nz // PATCH_Z
    width = PATCH_Z * nz
    features = PATCH_Z * rows
    tokens = slabs * bands_in * cells
    lane = jnp.arange(width, dtype=jnp.int32)
    j, pz, z = (lane // nz, lane % nz // PATCH_Z, lane % PATCH_Z)
    perm = ((z * nz + j * cells + pz)[:, None] == lane[None]).astype(bf16)
    order = feature_order(features).T
    vmem = pl.BlockSpec(memory_space=pltpu.VMEM)
    return pl.pallas_call(
        partial(patch_kernel, slabs=slabs, bands_in=bands_in),
        out_shape=[jax.ShapeDtypeStruct((features, tokens), bf16)] * 2,
        in_specs=[pl.BlockSpec(memory_space=pltpu.SMEM)] + [vmem] * (slabs + 2),
        out_specs=[vmem] * 2,
        scratch_shapes=[pltpu.VMEM((slabs, rows * bands_in, nz), bf16)],
        compiler_params=pltpu.CompilerParams(vmem_limit_bytes=12 * MIB),
        cost_estimate=pl.CostEstimate(flops=1_000_000_000, bytes_accessed=5_000_000, transcendentals=0),
        name="patchify",
    )(scalars, *blocks, perm, order)


def turn_kernel(scalars, cot_ref, own_ref, other_ref, held):
    per, hidden = own_ref.shape[:2]
    held[...] = cot_ref[...].T
    me, core = (scalars[0], scalars[1])
    for i in range(per):
        slot = (me % per) ^ i
        start = 2 * i * hidden
        own_ref[slot] = held[pl.ds(pl.multiple_of(start + core * hidden, hidden), hidden), :]
        other_ref[slot] = held[pl.ds(pl.multiple_of(start + (1 - core) * hidden, hidden), hidden), :]


def turn(cotangent, scalars, blocks):
    tokens, hidden = cotangent.shape
    width = hidden // blocks
    per = 1
    while per * width % 128:
        per *= 2
    out = jax.ShapeDtypeStruct((blocks, width // 2, tokens), bf16)
    out_spec = pl.BlockSpec((per, width // 2, tokens), lambda i, s: ((s[0] // per) ^ i, 0, 0))
    return pl.pallas_call(
        turn_kernel,
        out_shape=[out, out],
        grid_spec=pltpu.PrefetchScalarGridSpec(
            num_scalar_prefetch=1,
            grid=(blocks // per,),
            in_specs=[pl.BlockSpec((tokens, per * width), lambda i, s: (0, i))],
            out_specs=[out_spec, out_spec],
            scratch_shapes=[pltpu.VMEM((per * width, tokens), bf16)],
        ),
        cost_estimate=pl.CostEstimate(flops=0, bytes_accessed=6_300_000, transcendentals=0),
        name="turn",
    )(scalars, cotangent)


def embed_kernel(w_ref, patch_ref, normed_ref, embed_ref, inverse_ref):
    model, tokens = embed_ref.shape
    tile = min(tokens, 256)
    for i in range(0, tokens, tile):
        cols = pl.ds(i, tile)
        value = jnp.dot(w_ref[...], patch_ref[:, cols], preferred_element_type=f32).astype(bf16)
        embed_ref[:, cols] = value
        wide = value.astype(f32)
        total = jnp.sum(wide * wide, axis=0, keepdims=True)
        inverse = lax.rsqrt(total / model + epsilon)
        inverse_ref[:, cols] = inverse
        normed_ref[:, cols] = (wide * inverse).astype(bf16)


def embed(w_all, patches):
    model, features = w_all.shape
    tokens = patches.shape[1]
    vmem = pl.BlockSpec(memory_space=pltpu.VMEM)
    return pl.pallas_call(
        embed_kernel,
        out_shape=[
            jax.ShapeDtypeStruct((model, tokens), bf16),
            jax.ShapeDtypeStruct((model, tokens), bf16),
            jax.ShapeDtypeStruct((1, tokens), f32),
        ],
        in_specs=[vmem] * 2,
        out_specs=[vmem] * 3,
        compiler_params=pltpu.CompilerParams(vmem_limit_bytes=16 * MIB),
        cost_estimate=pl.CostEstimate(
            flops=2 * model * features * tokens, bytes_accessed=6_000_000, transcendentals=0
        ),
        name="embed",
    )(w_all, patches)


def join_kernel(scalars, *refs, slots):
    mine, (theirs, order_ref, out_ref, held) = (refs[:slots], refs[slots:])
    rows = mine[0].shape[0]
    me, core = (scalars[0], scalars[1])
    for k in range(slots):
        start = (me ^ k) * (2 * rows)
        held[pl.ds(pl.multiple_of(start + core * rows, 8), rows), :] = mine[k][...].astype(f32)
        held[pl.ds(pl.multiple_of(start + (1 - core) * rows, 8), rows), :] = theirs[k].astype(f32)
    out_ref[...] = jnp.dot(held[...].astype(bf16), order_ref[...], preferred_element_type=f32).astype(bf16)


def join(mine, theirs, scalars):
    slots = len(mine)
    rows, features = mine[0].shape
    order = feature_order(features).T
    vmem = pl.BlockSpec(memory_space=pltpu.VMEM)
    return pl.pallas_call(
        partial(join_kernel, slots=slots),
        out_shape=jax.ShapeDtypeStruct((2 * slots * rows, features), bf16),
        in_specs=[pl.BlockSpec(memory_space=pltpu.SMEM)] + [vmem] * (slots + 2),
        out_specs=vmem,
        scratch_shapes=[pltpu.VMEM((2 * slots * rows, features), f32)],
        compiler_params=pltpu.CompilerParams(vmem_limit_bytes=20 * MIB),
        cost_estimate=pl.CostEstimate(flops=1_700_000_000, bytes_accessed=5_000_000, transcendentals=0),
        name="join",
    )(scalars, *mine, theirs, order)


def tail_kernel(scalars, own_ref, far_ref, embed_ref, inverse_ref, plain_ref, *rest, slots):
    mine, (theirs, total, held) = (rest[:slots], rest[slots:])
    model = own_ref.shape[0]
    rows = model // (2 * slots)
    me, core = (scalars[0], scalars[1])
    inverse = inverse_ref[...]
    summed = own_ref[...] + far_ref[...].astype(f32)
    wide = embed_ref[...].astype(f32) * inverse
    inner = jnp.sum(summed * wide, axis=0, keepdims=True) / model
    total[...] = inverse * (summed - wide * inner)
    for k in range(slots):
        start = (me ^ k) * (2 * rows)
        for part in range(2):
            source = start + (core if part == 0 else 1 - core) * rows
            held[pl.ds((part * slots + k) * rows, rows), :] = total[pl.ds(pl.multiple_of(source, 8), rows), :]
    for part in (1, 0):
        grad = contract(
            held[pl.ds(part * slots * rows, slots * rows), :].astype(bf16), plain_ref[...], 1, 1
        ).astype(bf16)
        if part:
            theirs[...] = grad
        else:
            for k in range(slots):
                mine[k][...] = grad[k * rows : (k + 1) * rows]


def tail(own_grad, far_grad, embedded, inverse, plain, scalars, slots):
    model, tokens = own_grad.shape
    features = plain.shape[0]
    rows = model // (2 * slots)
    vmem = pl.BlockSpec(memory_space=pltpu.VMEM)
    return pl.pallas_call(
        partial(tail_kernel, slots=slots),
        out_shape=[jax.ShapeDtypeStruct((rows, features), bf16)] * slots
        + [jax.ShapeDtypeStruct((slots * rows, features), bf16)],
        in_specs=[pl.BlockSpec(memory_space=pltpu.SMEM)] + [vmem] * 5,
        out_specs=[vmem] * (slots + 1),
        scratch_shapes=[pltpu.VMEM((model, tokens), f32)] * 2,
        compiler_params=pltpu.CompilerParams(vmem_limit_bytes=28 * MIB),
        cost_estimate=pl.CostEstimate(flops=1_200_000_000, bytes_accessed=9_000_000, transcendentals=0),
        name="tail",
    )(scalars, own_grad, far_grad, embedded, inverse, plain)


def gelu_slope(value):
    scale = math.sqrt(2.0 / math.pi)
    square = value * value
    bend = jnp.tanh(value * (scale + (scale * 0.044715) * square))
    return 0.5 * (1.0 + bend) + 0.5 * value * (1.0 - bend * bend) * (
        scale + (3.0 * scale * 0.044715) * square
    )


def mlp_kernel(*refs, count):
    w_refs, (normed_own, normed_far, cot_own, cot_far), outs = (
        refs[:count],
        refs[count : count + 4],
        refs[count + 4 :],
    )
    act_own, act_far, w_out = outs[:3]
    grads = outs[3:]
    hidden, model = w_refs[0].shape
    tokens = normed_own.shape[1]
    for k in range(count):
        w_out[pl.ds(k * hidden, hidden), :] = w_refs[k][...]
    tile = min(tokens, 256)
    for normed, cot, act in ((normed_own, cot_own, act_own), (normed_far, cot_far, act_far)):
        for i in range(0, tokens, tile):
            cols = pl.ds(i, tile)
            pre_act = jnp.dot(w_out[...], normed[:, cols], preferred_element_type=f32)
            cots = jnp.concatenate([cot[k, :, cols] for k in range(count)], axis=0).astype(f32)
            act[:, cols] = (cots * gelu_slope(pre_act)).astype(bf16)
    for i in range(0, model, 256):
        cols = pl.ds(i, min(256, model - i))
        value = contract(act_own[...], normed_own[cols, :], 1, 1)
        value = (value + contract(act_far[...], normed_far[cols, :], 1, 1)).astype(bf16)
        for k in range(count):
            grads[k][:, cols] = value[k * hidden : (k + 1) * hidden]


def mlp(w_slots, normed, cots, part):
    count = len(w_slots)
    hidden, model = w_slots[0].shape
    tokens = normed[0].shape[1]
    vmem = pl.BlockSpec(memory_space=pltpu.VMEM)
    cot_spec = pl.BlockSpec((count, hidden, tokens), lambda i: (part, 0, 0))
    whole = pl.BlockSpec((model, tokens), lambda i: (0, 0))
    slot = pl.BlockSpec((hidden, model), lambda i: (0, 0))
    wide = pl.BlockSpec((count * hidden, tokens), lambda i: (0, 0))
    return pl.pallas_call(
        partial(mlp_kernel, count=count),
        grid=(1,),
        out_shape=[jax.ShapeDtypeStruct((count * hidden, tokens), bf16)] * 2
        + [jax.ShapeDtypeStruct((count * hidden, model), bf16)]
        + [jax.ShapeDtypeStruct((hidden, model), bf16)] * count,
        in_specs=[slot] * count + [whole] * 2 + [cot_spec] * 2,
        out_specs=[wide] * 2 + [pl.BlockSpec((count * hidden, model), lambda i: (0, 0))] + [slot] * count,
        compiler_params=pltpu.CompilerParams(vmem_limit_bytes=30 * MIB),
        cost_estimate=pl.CostEstimate(
            flops=8 * count * hidden * model * tokens, bytes_accessed=15_000_000, transcendentals=0
        ),
    )(*w_slots, *normed, *cots)


def bits_of(size):
    return [1 << i for i in range(size.bit_length() - 1)]


def gather_slots(shard, axis, order):
    slots = {0: shard}
    for bit in order:
        for k in list(slots):
            slots[k ^ bit] = exchange(slots[k], axis, bit)
    return [slots[k] for k in range(len(slots))]


def near_slots(shard, axis):
    slots = [shard]
    for k in range(2, lax.axis_size(axis), 2):
        slots += [None, exchange(shard, axis, k)]
    pairs = [exchange(slot, axis, 1) for slot in slots[::2]]
    return [slot for both in zip(slots[::2], pairs) for slot in both]


def scatter_slots(slots, axis, order):
    live = dict(enumerate(slots))
    for bit in order:
        for k in sorted(k for k in live if k & bit):
            arrived = exchange(live.pop(k), axis, bit)
            total = live[k ^ bit].astype(f32) + arrived.astype(f32)
            live[k ^ bit] = total if bit == order[-1] else total.astype(bf16)
    return live[0]


def swap(value):
    return exchange(value, "rve", 1)


def local(phase, load_case, moduli, loading_table, w_embed, w_up, cotangent):
    phase = phase[0]
    slab, ny, _ = phase.shape
    devs = lax.axis_size("dev")
    bits = bits_of(devs)
    me = lax.axis_index("dev")
    core = lax.axis_index("rve")
    features = w_embed.shape[1]
    rows_embed = w_embed.shape[0]
    tokens = cotangent.shape[0]
    bands_in = ny // devs // PATCH_Y
    grad_scale = 1.0 / math.sqrt(tokens * devs * 2)

    small = phase.astype(bf16)
    up = [(i, i + 1) for i in range(devs - 1)]
    down = [(j, i) for i, j in up]
    before = lax.ppermute(small[slab - SWEEPS :], "dev", up)
    after = lax.ppermute(small[:SWEEPS], "dev", down)

    scalars = jnp.stack([me, core, load_case[0]]).astype(jnp.int32)
    outs = solve(phase, before, after, scalars, moduli, loading_table, devs)
    displace, blocks = (outs[0], outs[1:])

    embed_slots = near_slots(w_embed, "dev")
    w_all = join(embed_slots, swap(jnp.stack(embed_slots)), scalars)

    up_slots = gather_slots(w_up, "dev", bits[::-1])
    cot_own, cot_other = turn(cotangent, scalars, devs)
    cots = (cot_own, swap(cot_other))

    arrived = [blocks[0]] + [exchange(blocks[k], "dev", k) for k in range(1, devs)]
    patches, plain = patchify(arrived, scalars, bands_in)
    far_patches = swap(patches)
    normed_own, embedded, inverse_rms = embed(w_all, patches)
    normed_far, _, _ = embed(w_all, far_patches)

    half = devs // 2
    grads = [None] * devs
    own_parts, far_parts, w_parts = ([], [], [])
    for part in (1, 0):
        act_own, act_far, w_part, *grads[part * half : (part + 1) * half] = mlp(
            up_slots[part * half : (part + 1) * half], (normed_own, normed_far), cots, part
        )
        own_parts.append(act_own)
        far_parts.append(act_far)
        w_parts.append(w_part)
    grad_up = scatter_slots(grads, "dev", bits) * grad_scale

    far_grad = sum(contract(w, act, 0, 0) for w, act in zip(w_parts, far_parts)).astype(bf16)
    partner = swap(far_grad)
    own_grad = sum(contract(w, act, 0, 0) for w, act in zip(w_parts, own_parts))
    *mine, yours = tail(own_grad, partner, embedded, inverse_rms, plain, scalars, devs)
    arrived = swap(yours).reshape(devs, rows_embed, features)
    mine = [(m.astype(f32) + arrived[k].astype(f32)).astype(bf16) for k, m in enumerate(mine)]
    grad_embed = scatter_slots(mine, "dev", bits[1::-1] + bits[2:]) * grad_scale
    return (displace[None], grad_embed, grad_up)


def solution(mesh):
    return jax.shard_map(
        local,
        mesh=mesh,
        in_specs=(
            P(("groups", "rve"), "dev", None, None),
            P(("groups", "rve")),
            P(),
            P(),
            P(("dev", "rve"), None),
            P(("dev", "rve"), None),
            P(("groups", "dev", "rve"), None),
        ),
        out_specs=(
            P(("groups", "rve"), None, "dev", None, None),
            P(("groups", "dev", "rve"), None),
            P(("groups", "dev", "rve"), None),
        ),
        check_vma=False,
    )
```

```python
from functools import partial
import math

import jax
import jax.numpy as jnp
from jax import lax
from jax.experimental import pallas as pl
from jax.experimental.pallas import tpu as pltpu
from jax.sharding import PartitionSpec as P


PATCH_Y = 8
PATCH_Z = 4
SWEEPS = 4


epsilon = 1e-06
bf16 = jnp.bfloat16
f32 = jnp.float32
MIB = 1024 * 1024


def contract(left, right, left_dim, right_dim):
    return lax.dot_general(
        left, right, (((left_dim,), (right_dim,)), ((), ())), preferred_element_type=f32
    )


def exchange(value, axis, bit):
    size = lax.axis_size(axis)
    return lax.ppermute(value, axis, [(i, i ^ bit) for i in range(size)])


def shifted(plane, axis, step):
    return pltpu.roll(plane, step % plane.shape[axis], axis)


def solver_kernel(
    scalars, tables, loading, phase_ref, before_ref, after_ref, displace_ref, *rest, slab, bands, patch_y
):
    block_refs = rest[:bands]
    key, face, self_x, rdiag, force, even, odd = rest[bands:]
    halo = SWEEPS
    total = slab + 2 * halo
    phases = tables.shape[1]
    me, case = (scalars[0], scalars[2])
    first_row, grid_rows = (me * slab, slab * bands)
    ny, nz = phase_ref.shape[1:]
    iota_y = lax.broadcasted_iota(jnp.int32, (ny, nz), 0)
    iota_z = lax.broadcasted_iota(jnp.int32, (ny, nz), 1)
    pairs = [(p, q) for p in range(phases) for q in range(p, phases)]

    def blend(kind, p, q):
        here, there = (jnp.full((1, nz), tables[kind, i], f32) for i in (p, q))
        return here if p == q else 2.0 * here * there / (here + there)

    values = {(kind, p, q): blend(kind, p, q) for p, q in pairs for kind in range(2)}

    def power(labels):
        result = jnp.full(labels.shape, 1, jnp.int32)
        for p in range(1, phases):
            result = jnp.where(labels == p, 1 << p, result)
        return result

    key[pl.ds(halo, slab)] = power(phase_ref[...])
    key[pl.ds(0, halo)] = power(before_ref[...].astype(f32).astype(jnp.int32))
    key[pl.ds(halo + slab, halo)] = power(after_ref[...].astype(f32).astype(jnp.int32))

    @pl.when(first_row == 0)
    def _():
        key[halo - 1] = key[halo]

    @pl.when(first_row + slab == grid_rows)
    def _():
        key[halo + slab] = key[halo + slab - 1]

    def faces(here, there):
        code = here + there
        results = [jnp.broadcast_to(values[kind, 0, 0], code.shape) for kind in range(2)]
        for p, q in pairs[1:]:
            hit = code == ((1 << p) + (1 << q))
            for kind in range(2):
                results[kind] = jnp.where(hit, values[kind, p, q], results[kind])
        return results

    def x_faces(row, carry):
        for kind, value in enumerate(faces(key[row], key[row + 1])):
            self_x[kind, row] = value
        return carry

    lax.fori_loop(0, total - 1, x_faces, 0)

    strain = [[loading[case, c, a] for a in range(3)] for c in range(3)]

    def setup(row, carry):
        here = key[row]
        own = faces(here, here)
        above_y = jnp.where(iota_y == ny - 1, here, shifted(here, 0, -1))
        above_z = jnp.where(iota_z == nz - 1, here, shifted(here, 1, -1))
        upper_y = faces(here, above_y)
        upper_z = faces(here, above_z)
        gaps, sums = ([], [])
        for kind in range(2):
            face[kind, 0, row] = jnp.where(iota_y == ny - 1, 0.0, upper_y[kind])
            face[kind, 1, row] = jnp.where(iota_z == nz - 1, 0.0, upper_z[kind])
            lower_y = jnp.where(iota_y == 0, own[kind], shifted(upper_y[kind], 0, 1))
            lower_z = jnp.where(iota_z == 0, own[kind], shifted(upper_z[kind], 1, 1))
            upper_x, lower_x = (self_x[kind, row], self_x[kind, row - 1])
            gaps.append([upper_x - lower_x, upper_y[kind] - lower_y, upper_z[kind] - lower_z])
            sums.append([upper_x + lower_x, upper_y[kind] + lower_y, upper_z[kind] + lower_z])
        global_row = first_row + row - halo
        inside = jnp.where((global_row >= 0) & (global_row < grid_rows), 1.0, 0.0)
        for c in range(3):
            kinds = [1 if a == c else 0 for a in range(3)]
            forcing = sum(strain[c][a] * gaps[kinds[a]][a] for a in range(3))
            diagonal = sums[kinds[0]][0] + sums[kinds[1]][1] + sums[kinds[2]][2]
            inverse = inside / diagonal
            rdiag[c, row] = inverse
            force[c, row] = forcing
            even[c, row] = forcing * inverse
        return carry

    lax.fori_loop(1, total - 1, setup, 0)

    buffers = (even, odd)
    for step in range(1, SWEEPS):
        source, target = (buffers[(step - 1) % 2], buffers[step % 2])

        def sweep(row, carry, source=source, target=target, last=step == SWEEPS - 1):
            for c in range(3):
                kx, ky, kz = (1 if a == c else 0 for a in range(3))
                here = source[c, row]
                face_y = face[ky, 0, row]
                face_z = face[kz, 1, row]
                summed = (
                    force[c, row]
                    + self_x[kx, row] * source[c, row + 1]
                    + self_x[kx, row - 1] * source[c, row - 1]
                    + face_y * shifted(here, 0, -1)
                    + shifted(face_y * here, 0, 1)
                    + face_z * shifted(here, 1, -1)
                    + shifted(face_z * here, 1, 1)
                )
                value = summed * rdiag[c, row]
                target[c, row] = value
                if last:
                    displace_ref[c, row - halo] = value
            return carry

        lax.fori_loop(1 + step, total - 1 - step, sweep, 0)

    band_rows = ny // bands
    for k in range(bands):
        band = me ^ k
        at = 0
        for b in range(band_rows // patch_y):
            start = pl.multiple_of(band * band_rows + b * patch_y, patch_y)
            for c in range(3):
                for x in range(0, slab, 2):
                    pair = jnp.concatenate(
                        [displace_ref[c, x + i, pl.ds(start, patch_y), :] for i in range(2)], axis=0
                    )
                    block_refs[k][pl.ds(at, 2 * patch_y), :] = pair.astype(bf16)
                    at += 2 * patch_y


def solve(phase, before, after, scalars, tables, loading, bands):
    slab, ny, nz = phase.shape
    total = slab + 2 * SWEEPS
    rows = 3 * slab * ny // bands
    smem = pl.BlockSpec(memory_space=pltpu.SMEM)
    vmem = pl.BlockSpec(memory_space=pltpu.VMEM)
    plane = (ny, nz)
    return pl.pallas_call(
        partial(solver_kernel, slab=slab, bands=bands, patch_y=PATCH_Y),
        out_shape=[jax.ShapeDtypeStruct((3, slab) + plane, f32)]
        + [jax.ShapeDtypeStruct((rows, nz), bf16)] * bands,
        in_specs=[smem, smem, smem, vmem, vmem, vmem],
        out_specs=[vmem] * (1 + bands),
        scratch_shapes=[
            pltpu.VMEM((total,) + plane, jnp.int32),
            pltpu.VMEM((2, 2, total) + plane, f32),
            pltpu.VMEM((2, total) + plane, f32),
            pltpu.VMEM((3, total) + plane, f32),
            pltpu.VMEM((3, total) + plane, f32),
            pltpu.VMEM((3, total) + plane, f32),
            pltpu.VMEM((3, total) + plane, f32),
        ],
        compiler_params=pltpu.CompilerParams(vmem_limit_bytes=30 * MIB),
        cost_estimate=pl.CostEstimate(flops=40_000_000, bytes_accessed=4_000_000, transcendentals=0),
        name="solver",
    )(scalars, tables, loading, phase, before, after)


def feature_order(features):
    feature = jnp.arange(features, dtype=jnp.int32)
    source = (feature % PATCH_Z) * (features // PATCH_Z) + feature // PATCH_Z
    return (feature[:, None] == source[None]).astype(bf16)


def patch_kernel(scalars, *refs, slabs, bands_in):
    block_refs, (perm_ref, order_ref, out_ref, plain_ref, held) = (refs[:slabs], refs[slabs:])
    rows, lanes = block_refs[0].shape
    rows = rows // bands_in
    me = scalars[0]
    for k in range(slabs):
        held[k] = block_refs[k][...]
    group = PATCH_Z
    for g in range(slabs * bands_in // group):
        parts = []
        for j in range(group):
            b, px = divmod(group * g + j, slabs)
            parts.append(held[me ^ px, pl.ds(b * rows, rows), :])
        moved = jnp.dot(
            jnp.concatenate(parts, axis=1), perm_ref[...], preferred_element_type=f32
        ).astype(bf16)
        for z in range(group):
            out_ref[pl.ds(z * rows, rows), pl.ds(g * lanes, lanes)] = moved[:, z * lanes : (z + 1) * lanes]
    plain_ref[...] = jnp.dot(order_ref[...], out_ref[...], preferred_element_type=f32).astype(bf16)


def patchify(blocks, scalars, bands_in):
    slabs = len(blocks)
    rows, nz = blocks[0].shape
    rows = rows // bands_in
    cells = nz // PATCH_Z
    width = PATCH_Z * nz
    features = PATCH_Z * rows
    tokens = slabs * bands_in * cells
    lane = jnp.arange(width, dtype=jnp.int32)
    j, pz, z = (lane // nz, lane % nz // PATCH_Z, lane % PATCH_Z)
    perm = ((z * nz + j * cells + pz)[:, None] == lane[None]).astype(bf16)
    order = feature_order(features).T
    vmem = pl.BlockSpec(memory_space=pltpu.VMEM)
    return pl.pallas_call(
        partial(patch_kernel, slabs=slabs, bands_in=bands_in),
        out_shape=[jax.ShapeDtypeStruct((features, tokens), bf16)] * 2,
        in_specs=[pl.BlockSpec(memory_space=pltpu.SMEM)] + [vmem] * (slabs + 2),
        out_specs=[vmem] * 2,
        scratch_shapes=[pltpu.VMEM((slabs, rows * bands_in, nz), bf16)],
        compiler_params=pltpu.CompilerParams(vmem_limit_bytes=12 * MIB),
        cost_estimate=pl.CostEstimate(flops=1_000_000_000, bytes_accessed=5_000_000, transcendentals=0),
        name="patchify",
    )(scalars, *blocks, perm, order)


def turn_kernel(scalars, cot_ref, own_ref, other_ref, held):
    per, hidden = own_ref.shape[:2]
    held[...] = cot_ref[...].T
    me, core = (scalars[0], scalars[1])
    for i in range(per):
        slot = (me % per) ^ i
        start = 2 * i * hidden
        own_ref[slot] = held[pl.ds(pl.multiple_of(start + core * hidden, hidden), hidden), :]
        other_ref[slot] = held[pl.ds(pl.multiple_of(start + (1 - core) * hidden, hidden), hidden), :]


def turn(cotangent, scalars, blocks, part):
    tokens, hidden = cotangent.shape
    width = hidden // blocks
    per = 1
    while per * width % 128:
        per *= 2
    steps = blocks // 2 // per
    out = jax.ShapeDtypeStruct((blocks // 2, width // 2, tokens), bf16)
    out_spec = pl.BlockSpec((per, width // 2, tokens), lambda i, s: (i, 0, 0))
    return pl.pallas_call(
        turn_kernel,
        out_shape=[out, out],
        grid_spec=pltpu.PrefetchScalarGridSpec(
            num_scalar_prefetch=1,
            grid=(steps,),
            in_specs=[
                pl.BlockSpec((tokens, per * width), lambda i, s: (0, (s[0] // per) ^ (part * steps + i)))
            ],
            out_specs=[out_spec, out_spec],
            scratch_shapes=[pltpu.VMEM((per * width, tokens), bf16)],
        ),
        compiler_params=pltpu.CompilerParams(vmem_limit_bytes=16 * MIB),
        cost_estimate=pl.CostEstimate(flops=0, bytes_accessed=3_200_000, transcendentals=0),
    )(scalars, cotangent)


def embed_kernel(w_ref, patch_ref, normed_ref, embed_ref, inverse_ref):
    model, tokens = embed_ref.shape
    tile = min(tokens, 256)
    for i in range(0, tokens, tile):
        cols = pl.ds(i, tile)
        value = jnp.dot(w_ref[...], patch_ref[:, cols], preferred_element_type=f32).astype(bf16)
        embed_ref[:, cols] = value
        wide = value.astype(f32)
        total = jnp.sum(wide * wide, axis=0, keepdims=True)
        inverse = lax.rsqrt(total / model + epsilon)
        inverse_ref[:, cols] = inverse
        normed_ref[:, cols] = (wide * inverse).astype(bf16)


def embed(w_all, patches):
    model, features = w_all.shape
    tokens = patches.shape[1]
    vmem = pl.BlockSpec(memory_space=pltpu.VMEM)
    return pl.pallas_call(
        embed_kernel,
        out_shape=[
            jax.ShapeDtypeStruct((model, tokens), bf16),
            jax.ShapeDtypeStruct((model, tokens), bf16),
            jax.ShapeDtypeStruct((1, tokens), f32),
        ],
        in_specs=[vmem] * 2,
        out_specs=[vmem] * 3,
        compiler_params=pltpu.CompilerParams(vmem_limit_bytes=16 * MIB),
        cost_estimate=pl.CostEstimate(
            flops=2 * model * features * tokens, bytes_accessed=6_000_000, transcendentals=0
        ),
        name="embed",
    )(w_all, patches)


def join_kernel(scalars, even, odd, even_far, odd_far, order_ref, out_ref, held):
    half, rows = even.shape[:2]
    me, core = (scalars[0], scalars[1])
    for k in range(2 * half):
        start = (me ^ k) * (2 * rows)
        for part, source in ((core, (even, odd)), (1 - core, (even_far, odd_far))):
            at = pl.multiple_of(start + part * rows, 8)
            held[pl.ds(at, rows), :] = source[k & 1][k // 2].astype(f32)
    out_ref[...] = jnp.dot(held[...].astype(bf16), order_ref[...], preferred_element_type=f32).astype(bf16)


def join(parts, scalars):
    half, rows, features = parts[0].shape
    order = feature_order(features).T
    vmem = pl.BlockSpec(memory_space=pltpu.VMEM)
    return pl.pallas_call(
        join_kernel,
        out_shape=jax.ShapeDtypeStruct((4 * half * rows, features), bf16),
        in_specs=[pl.BlockSpec(memory_space=pltpu.SMEM)] + [vmem] * 5,
        out_specs=vmem,
        scratch_shapes=[pltpu.VMEM((4 * half * rows, features), f32)],
        compiler_params=pltpu.CompilerParams(vmem_limit_bytes=20 * MIB),
        cost_estimate=pl.CostEstimate(flops=1_700_000_000, bytes_accessed=5_000_000, transcendentals=0),
        name="join",
    )(scalars, *parts, order)


def tail_kernel(scalars, own_ref, far_ref, embed_ref, inverse_ref, plain_ref, *rest, slots):
    mine, (theirs, total, held) = (rest[:slots], rest[slots:])
    model = own_ref.shape[0]
    rows = model // (2 * slots)
    me, core = (scalars[0], scalars[1])
    inverse = inverse_ref[...]
    summed = own_ref[...] + far_ref[...].astype(f32)
    wide = embed_ref[...].astype(f32) * inverse
    inner = jnp.sum(summed * wide, axis=0, keepdims=True) / model
    total[...] = inverse * (summed - wide * inner)
    for k in range(slots):
        start = (me ^ k) * (2 * rows)
        for part in range(2):
            source = start + (core if part == 0 else 1 - core) * rows
            held[pl.ds((part * slots + k) * rows, rows), :] = total[pl.ds(pl.multiple_of(source, 8), rows), :]
    for part in (1, 0):
        grad = contract(
            held[pl.ds(part * slots * rows, slots * rows), :].astype(bf16), plain_ref[...], 1, 1
        ).astype(bf16)
        if part:
            theirs[...] = grad
        else:
            for k in range(slots):
                mine[k][...] = grad[k * rows : (k + 1) * rows]


def tail(own_grad, far_grad, embedded, inverse, plain, scalars, slots):
    model, tokens = own_grad.shape
    features = plain.shape[0]
    rows = model // (2 * slots)
    vmem = pl.BlockSpec(memory_space=pltpu.VMEM)
    return pl.pallas_call(
        partial(tail_kernel, slots=slots),
        out_shape=[jax.ShapeDtypeStruct((rows, features), bf16)] * slots
        + [jax.ShapeDtypeStruct((slots * rows, features), bf16)],
        in_specs=[pl.BlockSpec(memory_space=pltpu.SMEM)] + [vmem] * 5,
        out_specs=[vmem] * (slots + 1),
        scratch_shapes=[pltpu.VMEM((model, tokens), f32)] * 2,
        compiler_params=pltpu.CompilerParams(vmem_limit_bytes=28 * MIB),
        cost_estimate=pl.CostEstimate(flops=1_200_000_000, bytes_accessed=9_000_000, transcendentals=0),
        name="tail",
    )(scalars, own_grad, far_grad, embedded, inverse, plain)


def gelu_slope(value):
    scale = math.sqrt(2.0 / math.pi)
    square = value * value
    bend = jnp.tanh(value * (scale + (scale * 0.044715) * square))
    return 0.5 * (1.0 + bend) + 0.5 * value * (1.0 - bend * bend) * (
        scale + (3.0 * scale * 0.044715) * square
    )


def mlp_kernel(scalars, *refs, picks, count):
    held = sum(picks)
    w_refs, (normed_own, normed_far, cot_own, cot_far), outs = (
        list(refs[:held]),
        refs[held : held + 4],
        refs[held + 4 :],
    )
    act_own, act_far, w_out = outs[:3]
    grads = outs[3:]
    model, tokens = normed_own.shape
    hidden = w_out.shape[0] // count
    for k in range(count):
        if picks[k] == 1:
            w_out[pl.ds(k * hidden, hidden), :] = w_refs.pop(0)[...]
            continue
        mid = hidden // 2
        for half in (scalars[3], 1 - scalars[3]):
            at = pl.multiple_of(k * hidden + half * mid, mid)
            w_out[pl.ds(at, mid), :] = w_refs.pop(0)[...]
    tile = min(tokens, 256)
    for normed, cot, act in ((normed_own, cot_own, act_own), (normed_far, cot_far, act_far)):
        for i in range(0, tokens, tile):
            cols = pl.ds(i, tile)
            pre_act = jnp.dot(w_out[...], normed[:, cols], preferred_element_type=f32)
            cots = jnp.concatenate([cot[k, :, cols] for k in range(count)], axis=0).astype(f32)
            act[:, cols] = (cots * gelu_slope(pre_act)).astype(bf16)
    for i in range(0, model, 256):
        cols = pl.ds(i, min(256, model - i))
        value = contract(act_own[...], normed_own[cols, :], 1, 1)
        value = (value + contract(act_far[...], normed_far[cols, :], 1, 1)).astype(bf16)
        rows = grads[0].shape[0]
        for k in range(len(grads)):
            grads[k][:, cols] = value[k * rows : (k + 1) * rows]


def mlp(scalars, w_slots, normed, cots, pieces):
    count = len(w_slots)
    picks = tuple(len(pieces) for pieces in w_slots)
    w_pieces = [piece for pieces in w_slots for piece in pieces]
    hidden, model = w_slots[0][0].shape
    tokens = normed[0].shape[1]
    vmem = pl.BlockSpec(memory_space=pltpu.VMEM)
    cot_spec = pl.BlockSpec((count, hidden, tokens), lambda i: (0, 0, 0))
    whole = pl.BlockSpec((model, tokens), lambda i: (0, 0))
    slot = pl.BlockSpec((hidden // pieces, model), lambda i: (0, 0))
    wide = pl.BlockSpec((count * hidden, tokens), lambda i: (0, 0))
    return pl.pallas_call(
        partial(mlp_kernel, picks=picks, count=count),
        grid=(1,),
        out_shape=[jax.ShapeDtypeStruct((count * hidden, tokens), bf16)] * 2
        + [jax.ShapeDtypeStruct((count * hidden, model), bf16)]
        + [jax.ShapeDtypeStruct((hidden // pieces, model), bf16)] * (count * pieces),
        in_specs=[pl.BlockSpec(memory_space=pltpu.SMEM)]
        + [pl.BlockSpec(piece.shape, lambda i: (0, 0)) for piece in w_pieces]
        + [whole] * 2
        + [cot_spec] * 2,
        out_specs=[wide] * 2 + [pl.BlockSpec((count * hidden, model), lambda i: (0, 0))] + [slot] * (count * pieces),
        compiler_params=pltpu.CompilerParams(vmem_limit_bytes=30 * MIB),
        cost_estimate=pl.CostEstimate(
            flops=8 * count * hidden * model * tokens, bytes_accessed=15_000_000, transcendentals=0
        ),
    )(scalars, *w_pieces, *normed, *cots)


def bits_of(size):
    return [1 << i for i in range(size.bit_length() - 1)]


def gather_slots(slots, axis, order):
    for bit in order:
        for k in list(slots):
            slots[k ^ bit] = exchange(slots[k], axis, bit)
    return [slots[k] for k in sorted(slots)]


def reduce_slots(live, axis, order):
    live = dict(live)
    for bit in order:
        for k in sorted(k for k in live if k & bit):
            arrived = exchange(live.pop(k), axis, bit)
            live[k ^ bit] = (live[k ^ bit].astype(f32) + arrived.astype(f32)).astype(bf16)
    (last,) = live.values()
    return last


def scatter_slots(slots, axis, bits):
    half = len(slots) // 2
    turned = bits[1::-1] + bits[2:-1] if len(slots[half]) > 1 else bits[:-1]
    near = reduce_slots({k: slots[k] for k in range(half)}, axis, turned)
    pieces = len(slots[half])
    sums = []
    for i in range(pieces):
        far = reduce_slots({k: slots[k][i] for k in range(half, 2 * half)}, axis, bits[:-1])
        arrived = exchange(far, axis, half)
        rows = far.shape[0]
        sums.append(near[i * rows : (i + 1) * rows].astype(f32) + arrived.astype(f32))
    return jnp.concatenate(sums, axis=0) if pieces > 1 else sums[0]


def swap(value):
    return exchange(value, "rve", 1)


def local(phase, load_case, moduli, loading_table, w_embed, w_up, cotangent):
    phase = phase[0]
    slab, ny, _ = phase.shape
    devs = lax.axis_size("dev")
    bits = bits_of(devs)
    me = lax.axis_index("dev")
    core = lax.axis_index("rve")
    parity = lax.axis_index("groups") % 2
    features = w_embed.shape[1]
    rows_embed = w_embed.shape[0]
    hidden = w_up.shape[0]
    tokens = cotangent.shape[0]
    bands_in = ny // devs // PATCH_Y
    grad_scale = 1.0 / math.sqrt(tokens * devs * 2)

    small = phase.astype(bf16)
    up = [(i, i + 1) for i in range(devs - 1)]
    down = [(j, i) for i, j in up]
    before = lax.ppermute(small[slab - SWEEPS :], "dev", up)
    after = lax.ppermute(small[:SWEEPS], "dev", down)

    scalars = jnp.stack([me, core, load_case[0], parity]).astype(jnp.int32)
    outs = solve(phase, before, after, scalars, moduli, loading_table, devs)
    displace, blocks = (outs[0], outs[1:])

    near = [w_embed] + [exchange(w_embed, "dev", k) for k in range(2, devs, 2)]
    even = jnp.stack(near)
    odd = exchange(even, "dev", 1)
    w_all = join((even, odd, swap(even), swap(odd)), scalars)

    mid = hidden // 2

    def mine(value):
        return lax.dynamic_slice_in_dim(value, parity * mid, mid, 0)

    near = exchange(mine(w_up), "dev", devs // 2)
    far = exchange(near, "groups", 1)
    top = jnp.concatenate(
        [jnp.where(parity == 0, near, far), jnp.where(parity == 0, far, near)], axis=0
    )
    up_even = gather_slots({0: w_up, devs // 2: top}, "dev", bits[-2:0:-1])
    up_slots = []
    for i, value in enumerate(up_even):
        k = 2 * i + 1
        if k in (1, devs - 1):
            up_slots += [(value,), (exchange(value, "dev", 1),)]
        else:
            rows = mine(value)
            near = exchange(rows, "dev", 1)
            up_slots += [(value,), (near, exchange(near, "groups", 1))]

    cots = []
    for part in range(2):
        cot_own, cot_other = turn(cotangent, scalars, devs, part)
        cots.append((cot_own, swap(cot_other)))

    arrived = [blocks[0]] + [exchange(blocks[k], "dev", k) for k in range(1, devs)]
    patches, plain = patchify(arrived, scalars, bands_in)
    far_patches = swap(patches)
    normed_own, embedded, inverse_rms = embed(w_all, patches)
    normed_far, _, _ = embed(w_all, far_patches)

    half = devs // 2
    grads = []
    own_parts, far_parts, w_parts = ([], [], [])
    for part in range(2):
        act_own, act_far, w_part, *outs = mlp(
            scalars, up_slots[part * half : (part + 1) * half], (normed_own, normed_far), cots[part], 1 + part
        )
        grads += [tuple(outs[2 * k : 2 * k + 2]) for k in range(half)] if part else outs
        own_parts.append(act_own)
        far_parts.append(act_far)
        w_parts.append(w_part)
    grad_up = scatter_slots(grads, "dev", bits) * grad_scale

    far_grad = sum(contract(w, act, 0, 0) for w, act in zip(w_parts, far_parts)).astype(bf16)
    partner = swap(far_grad)
    own_grad = sum(contract(w, act, 0, 0) for w, act in zip(w_parts, own_parts))
    *mine, yours = tail(own_grad, partner, embedded, inverse_rms, plain, scalars, devs)
    arrived = swap(yours).reshape(devs, rows_embed, features)
    mine = [(m.astype(f32) + arrived[k].astype(f32)).astype(bf16) for k, m in enumerate(mine)]
    grad_embed = scatter_slots(mine[:half] + [(m,) for m in mine[half:]], "dev", bits) * grad_scale
    return (displace[None], grad_embed, grad_up)


def solution(mesh):
    return jax.shard_map(
        local,
        mesh=mesh,
        in_specs=(
            P(("groups", "rve"), "dev", None, None),
            P(("groups", "rve")),
            P(),
            P(),
            P(("dev", "rve"), None),
            P(("dev", "rve"), None),
            P(("groups", "dev", "rve"), None),
        ),
        out_specs=(
            P(("groups", "rve"), None, "dev", None, None),
            P(("groups", "dev", "rve"), None),
            P(("groups", "dev", "rve"), None),
        ),
        check_vma=False,
    )
```

```python
from functools import partial
import math

import jax
import jax.numpy as jnp
from jax import lax
from jax.experimental import pallas as pl
from jax.experimental.pallas import tpu as pltpu
from jax.sharding import PartitionSpec as P


PATCH_Y = 8
PATCH_Z = 4
SWEEPS = 4


epsilon = 1e-06
bf16 = jnp.bfloat16
f32 = jnp.float32
MIB = 1024 * 1024


def contract(left, right, left_dim, right_dim):
    return lax.dot_general(
        left, right, (((left_dim,), (right_dim,)), ((), ())), preferred_element_type=f32
    )


def exchange(value, axis, bit):
    size = lax.axis_size(axis)
    return lax.ppermute(value, axis, [(i, i ^ bit) for i in range(size)])


def shifted(plane, axis, step):
    return pltpu.roll(plane, step % plane.shape[axis], axis)


def solver_kernel(
    scalars, tables, loading, phase_ref, before_ref, after_ref, displace_ref, *rest, slab, bands, patch_y
):
    block_refs = rest[:bands]
    key, face, self_x, rdiag, force, even, odd = rest[bands:]
    halo = SWEEPS
    total = slab + 2 * halo
    phases = tables.shape[1]
    me, case = (scalars[0], scalars[2])
    first_row, grid_rows = (me * slab, slab * bands)
    ny, nz = phase_ref.shape[1:]
    iota_y = lax.broadcasted_iota(jnp.int32, (ny, nz), 0)
    iota_z = lax.broadcasted_iota(jnp.int32, (ny, nz), 1)
    pairs = [(p, q) for p in range(phases) for q in range(p, phases)]

    def blend(kind, p, q):
        here, there = (jnp.full((1, nz), tables[kind, i], f32) for i in (p, q))
        return here if p == q else 2.0 * here * there / (here + there)

    values = {(kind, p, q): blend(kind, p, q) for p, q in pairs for kind in range(2)}

    def power(labels):
        result = jnp.full(labels.shape, 1, jnp.int32)
        for p in range(1, phases):
            result = jnp.where(labels == p, 1 << p, result)
        return result

    key[pl.ds(halo, slab)] = power(phase_ref[...])
    key[pl.ds(0, halo)] = power(before_ref[...].astype(f32).astype(jnp.int32))
    key[pl.ds(halo + slab, halo)] = power(after_ref[...].astype(f32).astype(jnp.int32))

    @pl.when(first_row == 0)
    def _():
        key[halo - 1] = key[halo]

    @pl.when(first_row + slab == grid_rows)
    def _():
        key[halo + slab] = key[halo + slab - 1]

    def faces(here, there):
        code = here + there
        results = [jnp.broadcast_to(values[kind, 0, 0], code.shape) for kind in range(2)]
        for p, q in pairs[1:]:
            hit = code == ((1 << p) + (1 << q))
            for kind in range(2):
                results[kind] = jnp.where(hit, values[kind, p, q], results[kind])
        return results

    def x_faces(row, carry):
        for kind, value in enumerate(faces(key[row], key[row + 1])):
            self_x[kind, row] = value
        return carry

    lax.fori_loop(0, total - 1, x_faces, 0)

    strain = [[loading[case, c, a] for a in range(3)] for c in range(3)]

    def setup(row, carry):
        here = key[row]
        own = [jnp.broadcast_to(values[kind, 0, 0], here.shape) for kind in range(2)]
        for p in range(1, phases):
            hit = here == (1 << p)
            own = [jnp.where(hit, values[kind, p, p], own[kind]) for kind in range(2)]
        above_y = jnp.where(iota_y == ny - 1, here, shifted(here, 0, -1))
        above_z = jnp.where(iota_z == nz - 1, here, shifted(here, 1, -1))
        upper_y = faces(here, above_y)
        upper_z = faces(here, above_z)
        gaps, sums = ([], [])
        for kind in range(2):
            face[kind, 0, row] = jnp.where(iota_y == ny - 1, 0.0, upper_y[kind])
            face[kind, 1, row] = jnp.where(iota_z == nz - 1, 0.0, upper_z[kind])
            lower_y = jnp.where(iota_y == 0, own[kind], shifted(upper_y[kind], 0, 1))
            lower_z = jnp.where(iota_z == 0, own[kind], shifted(upper_z[kind], 1, 1))
            upper_x, lower_x = (self_x[kind, row], self_x[kind, row - 1])
            gaps.append([upper_x - lower_x, upper_y[kind] - lower_y, upper_z[kind] - lower_z])
            sums.append([upper_x + lower_x, upper_y[kind] + lower_y, upper_z[kind] + lower_z])
        global_row = first_row + row - halo
        inside = jnp.where((global_row >= 0) & (global_row < grid_rows), 1.0, 0.0)
        for c in range(3):
            kinds = [1 if a == c else 0 for a in range(3)]
            forcing = sum(strain[c][a] * gaps[kinds[a]][a] for a in range(3))
            diagonal = sums[kinds[0]][0] + sums[kinds[1]][1] + sums[kinds[2]][2]
            inverse = inside / diagonal
            rdiag[c, row] = inverse
            force[c, row] = forcing
            even[c, row] = forcing * inverse
        return carry

    lax.fori_loop(1, total - 1, setup, 0, unroll=2)

    buffers = (even, odd)
    for step in range(1, SWEEPS):
        source, target = (buffers[(step - 1) % 2], buffers[step % 2])

        def sweep(row, carry, source=source, target=target, last=step == SWEEPS - 1):
            for c in range(3):
                kx, ky, kz = (1 if a == c else 0 for a in range(3))
                here = source[c, row]
                face_y = face[ky, 0, row]
                face_z = face[kz, 1, row]
                summed = (
                    force[c, row]
                    + self_x[kx, row] * source[c, row + 1]
                    + self_x[kx, row - 1] * source[c, row - 1]
                    + face_y * shifted(here, 0, -1)
                    + shifted(face_y * here, 0, 1)
                    + face_z * shifted(here, 1, -1)
                    + shifted(face_z * here, 1, 1)
                )
                value = summed * rdiag[c, row]
                target[c, row] = value
                if last:
                    displace_ref[c, row - halo] = value
            return carry

        lax.fori_loop(1 + step, total - 1 - step, sweep, 0, unroll=2)

    band_rows = ny // bands
    for k in range(bands):
        band = me ^ k
        at = 0
        for b in range(band_rows // patch_y):
            start = pl.multiple_of(band * band_rows + b * patch_y, patch_y)
            for c in range(3):
                for x in range(0, slab, 2):
                    pair = jnp.concatenate(
                        [displace_ref[c, x + i, pl.ds(start, patch_y), :] for i in range(2)], axis=0
                    )
                    block_refs[k][pl.ds(at, 2 * patch_y), :] = pair.astype(bf16)
                    at += 2 * patch_y


def solve(phase, before, after, scalars, tables, loading, bands):
    slab, ny, nz = phase.shape
    total = slab + 2 * SWEEPS
    rows = 3 * slab * ny // bands
    smem = pl.BlockSpec(memory_space=pltpu.SMEM)
    vmem = pl.BlockSpec(memory_space=pltpu.VMEM)
    plane = (ny, nz)
    return pl.pallas_call(
        partial(solver_kernel, slab=slab, bands=bands, patch_y=PATCH_Y),
        out_shape=[jax.ShapeDtypeStruct((3, slab) + plane, f32)]
        + [jax.ShapeDtypeStruct((rows, nz), bf16)] * bands,
        in_specs=[smem, smem, smem, vmem, vmem, vmem],
        out_specs=[vmem] * (1 + bands),
        scratch_shapes=[
            pltpu.VMEM((total,) + plane, jnp.int32),
            pltpu.VMEM((2, 2, total) + plane, f32),
            pltpu.VMEM((2, total) + plane, f32),
            pltpu.VMEM((3, total) + plane, f32),
            pltpu.VMEM((3, total) + plane, f32),
            pltpu.VMEM((3, total) + plane, f32),
            pltpu.VMEM((3, total) + plane, f32),
        ],
        compiler_params=pltpu.CompilerParams(vmem_limit_bytes=30 * MIB),
        cost_estimate=pl.CostEstimate(flops=40_000_000, bytes_accessed=4_000_000, transcendentals=0),
        name="solver",
    )(scalars, tables, loading, phase, before, after)


def feature_order(features):
    feature = jnp.arange(features, dtype=jnp.int32)
    source = (feature % PATCH_Z) * (features // PATCH_Z) + feature // PATCH_Z
    return (feature[:, None] == source[None]).astype(bf16)


def patch_kernel(scalars, *refs, slabs, bands_in):
    block_refs, (perm_ref, order_ref, out_ref, plain_ref, held) = (refs[:slabs], refs[slabs:])
    rows, lanes = block_refs[0].shape
    rows = rows // bands_in
    me = scalars[0]
    for k in range(slabs):
        held[k] = block_refs[k][...]
    group = PATCH_Z
    for g in range(slabs * bands_in // group):
        parts = []
        for j in range(group):
            b, px = divmod(group * g + j, slabs)
            parts.append(held[me ^ px, pl.ds(b * rows, rows), :])
        moved = jnp.dot(
            jnp.concatenate(parts, axis=1), perm_ref[...], preferred_element_type=f32
        ).astype(bf16)
        for z in range(group):
            out_ref[pl.ds(z * rows, rows), pl.ds(g * lanes, lanes)] = moved[:, z * lanes : (z + 1) * lanes]
    plain_ref[...] = jnp.dot(order_ref[...], out_ref[...], preferred_element_type=f32).astype(bf16)


def patchify(blocks, scalars, bands_in):
    slabs = len(blocks)
    rows, nz = blocks[0].shape
    rows = rows // bands_in
    cells = nz // PATCH_Z
    width = PATCH_Z * nz
    features = PATCH_Z * rows
    tokens = slabs * bands_in * cells
    lane = jnp.arange(width, dtype=jnp.int32)
    j, pz, z = (lane // nz, lane % nz // PATCH_Z, lane % PATCH_Z)
    perm = ((z * nz + j * cells + pz)[:, None] == lane[None]).astype(bf16)
    order = feature_order(features).T
    vmem = pl.BlockSpec(memory_space=pltpu.VMEM)
    return pl.pallas_call(
        partial(patch_kernel, slabs=slabs, bands_in=bands_in),
        out_shape=[jax.ShapeDtypeStruct((features, tokens), bf16)] * 2,
        in_specs=[pl.BlockSpec(memory_space=pltpu.SMEM)] + [vmem] * (slabs + 2),
        out_specs=[vmem] * 2,
        scratch_shapes=[pltpu.VMEM((slabs, rows * bands_in, nz), bf16)],
        compiler_params=pltpu.CompilerParams(vmem_limit_bytes=12 * MIB),
        cost_estimate=pl.CostEstimate(flops=1_000_000_000, bytes_accessed=5_000_000, transcendentals=0),
        name="patchify",
    )(scalars, *blocks, perm, order)


def turn_kernel(scalars, cot_ref, own_ref, other_ref, held):
    per, hidden = own_ref.shape[:2]
    held[...] = cot_ref[...].T
    me, core = (scalars[0], scalars[1])
    for i in range(per):
        slot = (me % per) ^ i
        start = 2 * i * hidden
        own_ref[slot] = held[pl.ds(pl.multiple_of(start + core * hidden, hidden), hidden), :]
        other_ref[slot] = held[pl.ds(pl.multiple_of(start + (1 - core) * hidden, hidden), hidden), :]


def turn(cotangent, scalars, blocks, part):
    tokens, hidden = cotangent.shape
    width = hidden // blocks
    per = 1
    while per * width % 128:
        per *= 2
    steps = blocks // 2 // per
    out = jax.ShapeDtypeStruct((blocks // 2, width // 2, tokens), bf16)
    out_spec = pl.BlockSpec((per, width // 2, tokens), lambda i, s: (i, 0, 0))
    return pl.pallas_call(
        turn_kernel,
        out_shape=[out, out],
        grid_spec=pltpu.PrefetchScalarGridSpec(
            num_scalar_prefetch=1,
            grid=(steps,),
            in_specs=[
                pl.BlockSpec((tokens, per * width), lambda i, s: (0, (s[0] // per) ^ (part * steps + i)))
            ],
            out_specs=[out_spec, out_spec],
            scratch_shapes=[pltpu.VMEM((per * width, tokens), bf16)],
        ),
        compiler_params=pltpu.CompilerParams(vmem_limit_bytes=16 * MIB),
        cost_estimate=pl.CostEstimate(flops=0, bytes_accessed=3_200_000, transcendentals=0),
    )(scalars, cotangent)


def embed_kernel(w_ref, patch_ref, normed_ref, embed_ref, inverse_ref):
    model, tokens = embed_ref.shape
    tile = min(tokens, 256)
    for i in range(0, tokens, tile):
        cols = pl.ds(i, tile)
        value = jnp.dot(w_ref[...], patch_ref[:, cols], preferred_element_type=f32).astype(bf16)
        embed_ref[:, cols] = value
        wide = value.astype(f32)
        total = jnp.sum(wide * wide, axis=0, keepdims=True)
        inverse = lax.rsqrt(total / model + epsilon)
        inverse_ref[:, cols] = inverse
        normed_ref[:, cols] = (wide * inverse).astype(bf16)


def embed(w_all, patches):
    model, features = w_all.shape
    tokens = patches.shape[1]
    vmem = pl.BlockSpec(memory_space=pltpu.VMEM)
    return pl.pallas_call(
        embed_kernel,
        out_shape=[
            jax.ShapeDtypeStruct((model, tokens), bf16),
            jax.ShapeDtypeStruct((model, tokens), bf16),
            jax.ShapeDtypeStruct((1, tokens), f32),
        ],
        in_specs=[vmem] * 2,
        out_specs=[vmem] * 3,
        compiler_params=pltpu.CompilerParams(vmem_limit_bytes=16 * MIB),
        cost_estimate=pl.CostEstimate(
            flops=2 * model * features * tokens, bytes_accessed=6_000_000, transcendentals=0
        ),
        name="embed",
    )(w_all, patches)


def join_kernel(scalars, even, odd, even_far, odd_far, order_ref, out_ref, held):
    half, rows = even.shape[:2]
    me, core = (scalars[0], scalars[1])
    for k in range(2 * half):
        start = (me ^ k) * (2 * rows)
        for part, source in ((core, (even, odd)), (1 - core, (even_far, odd_far))):
            at = pl.multiple_of(start + part * rows, 8)
            held[pl.ds(at, rows), :] = source[k & 1][k // 2].astype(f32)
    out_ref[...] = jnp.dot(held[...].astype(bf16), order_ref[...], preferred_element_type=f32).astype(bf16)


def join(parts, scalars):
    half, rows, features = parts[0].shape
    order = feature_order(features).T
    vmem = pl.BlockSpec(memory_space=pltpu.VMEM)
    return pl.pallas_call(
        join_kernel,
        out_shape=jax.ShapeDtypeStruct((4 * half * rows, features), bf16),
        in_specs=[pl.BlockSpec(memory_space=pltpu.SMEM)] + [vmem] * 5,
        out_specs=vmem,
        scratch_shapes=[pltpu.VMEM((4 * half * rows, features), f32)],
        compiler_params=pltpu.CompilerParams(vmem_limit_bytes=20 * MIB),
        cost_estimate=pl.CostEstimate(flops=1_700_000_000, bytes_accessed=5_000_000, transcendentals=0),
        name="join",
    )(scalars, *parts, order)


def tail_kernel(scalars, own_ref, far_ref, embed_ref, inverse_ref, plain_ref, *rest, slots):
    mine, (theirs, total, held) = (rest[:slots], rest[slots:])
    model = own_ref.shape[0]
    rows = model // (2 * slots)
    me, core = (scalars[0], scalars[1])
    inverse = inverse_ref[...]
    summed = own_ref[...] + far_ref[...].astype(f32)
    wide = embed_ref[...].astype(f32) * inverse
    inner = jnp.sum(summed * wide, axis=0, keepdims=True) / model
    total[...] = inverse * (summed - wide * inner)
    for k in range(slots):
        start = (me ^ k) * (2 * rows)
        for part in range(2):
            source = start + (core if part == 0 else 1 - core) * rows
            held[pl.ds((part * slots + k) * rows, rows), :] = total[pl.ds(pl.multiple_of(source, 8), rows), :]
    for part in (1, 0):
        grad = contract(
            held[pl.ds(part * slots * rows, slots * rows), :].astype(bf16), plain_ref[...], 1, 1
        ).astype(bf16)
        if part:
            theirs[...] = grad
        else:
            for k in range(slots):
                mine[k][...] = grad[k * rows : (k + 1) * rows]


def tail(own_grad, far_grad, embedded, inverse, plain, scalars, slots):
    model, tokens = own_grad.shape
    features = plain.shape[0]
    rows = model // (2 * slots)
    vmem = pl.BlockSpec(memory_space=pltpu.VMEM)
    return pl.pallas_call(
        partial(tail_kernel, slots=slots),
        out_shape=[jax.ShapeDtypeStruct((rows, features), bf16)] * slots
        + [jax.ShapeDtypeStruct((slots * rows, features), bf16)],
        in_specs=[pl.BlockSpec(memory_space=pltpu.SMEM)] + [vmem] * 5,
        out_specs=[vmem] * (slots + 1),
        scratch_shapes=[pltpu.VMEM((model, tokens), f32)] * 2,
        compiler_params=pltpu.CompilerParams(vmem_limit_bytes=28 * MIB),
        cost_estimate=pl.CostEstimate(flops=1_200_000_000, bytes_accessed=9_000_000, transcendentals=0),
        name="tail",
    )(scalars, own_grad, far_grad, embedded, inverse, plain)


def gelu_slope(value):
    scale = math.sqrt(2.0 / math.pi)
    square = value * value
    bend = jnp.tanh(value * (scale + (scale * 0.044715) * square))
    return 0.5 * (1.0 + bend) + 0.5 * value * (1.0 - bend * bend) * (
        scale + (3.0 * scale * 0.044715) * square
    )


def mlp_kernel(scalars, *refs, picks, count):
    held = sum(picks)
    w_refs, (normed_own, normed_far, cot_own, cot_far), outs = (
        list(refs[:held]),
        refs[held : held + 4],
        refs[held + 4 :],
    )
    act_own, act_far, w_out = outs[:3]
    grads = outs[3:]
    model, tokens = normed_own.shape
    hidden = w_out.shape[0] // count
    for k in range(count):
        if picks[k] == 1:
            w_out[pl.ds(k * hidden, hidden), :] = w_refs.pop(0)[...]
            continue
        mid = hidden // 2
        for half in (scalars[3], 1 - scalars[3]):
            at = pl.multiple_of(k * hidden + half * mid, mid)
            w_out[pl.ds(at, mid), :] = w_refs.pop(0)[...]
    tile = min(tokens, 256)
    for normed, cot, act in ((normed_own, cot_own, act_own), (normed_far, cot_far, act_far)):
        for i in range(0, tokens, tile):
            cols = pl.ds(i, tile)
            pre_act = jnp.dot(w_out[...], normed[:, cols], preferred_element_type=f32)
            cots = jnp.concatenate([cot[k, :, cols] for k in range(count)], axis=0).astype(f32)
            act[:, cols] = (cots * gelu_slope(pre_act)).astype(bf16)
    for i in range(0, model, 256):
        cols = pl.ds(i, min(256, model - i))
        value = contract(act_own[...], normed_own[cols, :], 1, 1)
        value = (value + contract(act_far[...], normed_far[cols, :], 1, 1)).astype(bf16)
        rows = grads[0].shape[0]
        for k in range(len(grads)):
            grads[k][:, cols] = value[k * rows : (k + 1) * rows]


def mlp(scalars, w_slots, normed, cots, pieces):
    count = len(w_slots)
    picks = tuple(len(pieces) for pieces in w_slots)
    w_pieces = [piece for pieces in w_slots for piece in pieces]
    hidden, model = w_slots[0][0].shape
    tokens = normed[0].shape[1]
    vmem = pl.BlockSpec(memory_space=pltpu.VMEM)
    cot_spec = pl.BlockSpec((count, hidden, tokens), lambda i: (0, 0, 0))
    whole = pl.BlockSpec((model, tokens), lambda i: (0, 0))
    slot = pl.BlockSpec((hidden // pieces, model), lambda i: (0, 0))
    wide = pl.BlockSpec((count * hidden, tokens), lambda i: (0, 0))
    return pl.pallas_call(
        partial(mlp_kernel, picks=picks, count=count),
        grid=(1,),
        out_shape=[jax.ShapeDtypeStruct((count * hidden, tokens), bf16)] * 2
        + [jax.ShapeDtypeStruct((count * hidden, model), bf16)]
        + [jax.ShapeDtypeStruct((hidden // pieces, model), bf16)] * (count * pieces),
        in_specs=[pl.BlockSpec(memory_space=pltpu.SMEM)]
        + [pl.BlockSpec(piece.shape, lambda i: (0, 0)) for piece in w_pieces]
        + [whole] * 2
        + [cot_spec] * 2,
        out_specs=[wide] * 2 + [pl.BlockSpec((count * hidden, model), lambda i: (0, 0))] + [slot] * (count * pieces),
        compiler_params=pltpu.CompilerParams(vmem_limit_bytes=30 * MIB),
        cost_estimate=pl.CostEstimate(
            flops=8 * count * hidden * model * tokens, bytes_accessed=15_000_000, transcendentals=0
        ),
    )(scalars, *w_pieces, *normed, *cots)


def bits_of(size):
    return [1 << i for i in range(size.bit_length() - 1)]


def gather_slots(slots, axis, order):
    for bit in order:
        for k in list(slots):
            slots[k ^ bit] = exchange(slots[k], axis, bit)
    return [slots[k] for k in sorted(slots)]


def reduce_slots(live, axis, order):
    live = dict(live)
    for bit in order:
        for k in sorted(k for k in live if k & bit):
            arrived = exchange(live.pop(k), axis, bit)
            live[k ^ bit] = (live[k ^ bit].astype(f32) + arrived.astype(f32)).astype(bf16)
    (last,) = live.values()
    return last


def scatter_slots(slots, axis, bits):
    half = len(slots) // 2
    turned = bits[1::-1] + bits[2:-1] if len(slots[half]) > 1 else bits[:-1]
    near = reduce_slots({k: slots[k] for k in range(half)}, axis, turned)
    pieces = len(slots[half])
    sums = []
    for i in range(pieces):
        far = reduce_slots({k: slots[k][i] for k in range(half, 2 * half)}, axis, bits[:-1])
        arrived = exchange(far, axis, half)
        rows = far.shape[0]
        sums.append(near[i * rows : (i + 1) * rows].astype(f32) + arrived.astype(f32))
    return jnp.concatenate(sums, axis=0) if pieces > 1 else sums[0]


def swap(value):
    return exchange(value, "rve", 1)


def local(phase, load_case, moduli, loading_table, w_embed, w_up, cotangent):
    phase = phase[0]
    slab, ny, _ = phase.shape
    devs = lax.axis_size("dev")
    bits = bits_of(devs)
    me = lax.axis_index("dev")
    core = lax.axis_index("rve")
    parity = lax.axis_index("groups") % 2
    features = w_embed.shape[1]
    rows_embed = w_embed.shape[0]
    hidden = w_up.shape[0]
    tokens = cotangent.shape[0]
    bands_in = ny // devs // PATCH_Y
    grad_scale = 1.0 / math.sqrt(tokens * devs * 2)

    small = phase.astype(bf16)
    up = [(i, i + 1) for i in range(devs - 1)]
    down = [(j, i) for i, j in up]
    before = lax.ppermute(small[slab - SWEEPS :], "dev", up)
    after = lax.ppermute(small[:SWEEPS], "dev", down)

    scalars = jnp.stack([me, core, load_case[0], parity]).astype(jnp.int32)
    outs = solve(phase, before, after, scalars, moduli, loading_table, devs)
    displace, blocks = (outs[0], outs[1:])

    near = [w_embed] + [exchange(w_embed, "dev", k) for k in range(2, devs, 2)]
    even = jnp.stack(near)
    odd = exchange(even, "dev", 1)
    w_all = join((even, odd, swap(even), swap(odd)), scalars)

    mid = hidden // 2

    def mine(value):
        return lax.dynamic_slice_in_dim(value, parity * mid, mid, 0)

    near = exchange(mine(w_up), "dev", devs // 2)
    far = exchange(near, "groups", 1)
    top = jnp.concatenate(
        [jnp.where(parity == 0, near, far), jnp.where(parity == 0, far, near)], axis=0
    )
    up_even = gather_slots({0: w_up, devs // 2: top}, "dev", bits[-2:0:-1])
    up_slots = []
    for i, value in enumerate(up_even):
        k = 2 * i + 1
        if k in (1, devs - 1):
            up_slots += [(value,), (exchange(value, "dev", 1),)]
        else:
            rows = mine(value)
            near = exchange(rows, "dev", 1)
            up_slots += [(value,), (near, exchange(near, "groups", 1))]

    cots = []
    for part in range(2):
        cot_own, cot_other = turn(cotangent, scalars, devs, part)
        cots.append((cot_own, swap(cot_other)))

    arrived = [blocks[0]] + [exchange(blocks[k], "dev", k) for k in range(1, devs)]
    patches, plain = patchify(arrived, scalars, bands_in)
    far_patches = swap(patches)
    normed_own, embedded, inverse_rms = embed(w_all, patches)
    normed_far, _, _ = embed(w_all, far_patches)

    half = devs // 2
    grads = []
    own_parts, far_parts, w_parts = ([], [], [])
    for part in range(2):
        act_own, act_far, w_part, *outs = mlp(
            scalars, up_slots[part * half : (part + 1) * half], (normed_own, normed_far), cots[part], 1 + part
        )
        grads += [tuple(outs[2 * k : 2 * k + 2]) for k in range(half)] if part else outs
        own_parts.append(act_own)
        far_parts.append(act_far)
        w_parts.append(w_part)
    grad_up = scatter_slots(grads, "dev", bits) * grad_scale

    far_grad = sum(contract(w, act, 0, 0) for w, act in zip(w_parts, far_parts)).astype(bf16)
    partner = swap(far_grad)
    own_grad = sum(contract(w, act, 0, 0) for w, act in zip(w_parts, own_parts))
    *mine, yours = tail(own_grad, partner, embedded, inverse_rms, plain, scalars, devs)
    arrived = swap(yours).reshape(devs, rows_embed, features)
    mine = [(m.astype(f32) + arrived[k].astype(f32)).astype(bf16) for k, m in enumerate(mine)]
    grad_embed = scatter_slots(mine[:half] + [(m,) for m in mine[half:]], "dev", bits) * grad_scale
    return (displace[None], grad_embed, grad_up)


def solution(mesh):
    return jax.shard_map(
        local,
        mesh=mesh,
        in_specs=(
            P(("groups", "rve"), "dev", None, None),
            P(("groups", "rve")),
            P(),
            P(),
            P(("dev", "rve"), None),
            P(("dev", "rve"), None),
            P(("groups", "dev", "rve"), None),
        ),
        out_specs=(
            P(("groups", "rve"), None, "dev", None, None),
            P(("groups", "dev", "rve"), None),
            P(("groups", "dev", "rve"), None),
        ),
        check_vma=False,
    )
```

```python
from functools import partial
import math

import jax
import jax.numpy as jnp
from jax import lax
from jax.experimental import pallas as pl
from jax.experimental.pallas import tpu as pltpu
from jax.sharding import PartitionSpec as P


PATCH_Y = 8
PATCH_Z = 4
SWEEPS = 4


epsilon = 1e-06
bf16 = jnp.bfloat16
f32 = jnp.float32
MIB = 1024 * 1024


def contract(left, right, left_dim, right_dim):
    return lax.dot_general(
        left, right, (((left_dim,), (right_dim,)), ((), ())), preferred_element_type=f32
    )


def exchange(value, axis, bit):
    size = lax.axis_size(axis)
    return lax.ppermute(value, axis, [(i, i ^ bit) for i in range(size)])


def shifted(plane, axis, step):
    return pltpu.roll(plane, step % plane.shape[axis], axis)


def solver_kernel(
    scalars, tables, loading, phase_ref, before_ref, after_ref, displace_ref, *rest, slab, bands, patch_y
):
    block_refs = rest[:bands]
    key, face, self_x, rdiag, force, even, odd = rest[bands:]
    halo = SWEEPS
    total = slab + 2 * halo
    phases = tables.shape[1]
    me, case = (scalars[0], scalars[2])
    first_row, grid_rows = (me * slab, slab * bands)
    ny, nz = phase_ref.shape[1:]
    iota_y = lax.broadcasted_iota(jnp.int32, (ny, nz), 0)
    iota_z = lax.broadcasted_iota(jnp.int32, (ny, nz), 1)
    pairs = [(p, q) for p in range(phases) for q in range(p, phases)]

    def blend(kind, p, q):
        here, there = (jnp.full((1, nz), tables[kind, i], f32) for i in (p, q))
        return here if p == q else 2.0 * here * there / (here + there)

    values = {(kind, p, q): blend(kind, p, q) for p, q in pairs for kind in range(2)}

    def power(labels):
        result = jnp.full(labels.shape, 1, jnp.int32)
        for p in range(1, phases):
            result = jnp.where(labels == p, 1 << p, result)
        return result

    key[pl.ds(halo, slab)] = power(phase_ref[...])
    key[pl.ds(0, halo)] = power(before_ref[...].astype(f32).astype(jnp.int32))
    key[pl.ds(halo + slab, halo)] = power(after_ref[...].astype(f32).astype(jnp.int32))

    @pl.when(first_row == 0)
    def _():
        key[halo - 1] = key[halo]

    @pl.when(first_row + slab == grid_rows)
    def _():
        key[halo + slab] = key[halo + slab - 1]

    def faces(here, there):
        code = here + there
        results = [jnp.broadcast_to(values[kind, 0, 0], code.shape) for kind in range(2)]
        for p, q in pairs[1:]:
            hit = code == ((1 << p) + (1 << q))
            for kind in range(2):
                results[kind] = jnp.where(hit, values[kind, p, q], results[kind])
        return results

    def x_faces(row, carry):
        for kind, value in enumerate(faces(key[row], key[row + 1])):
            self_x[kind, row] = value
        return carry

    lax.fori_loop(0, total - 1, x_faces, 0, unroll=3)

    strain = [[loading[case, c, a] for a in range(3)] for c in range(3)]

    def setup(row, carry):
        here = key[row]
        own = [jnp.broadcast_to(values[kind, 0, 0], here.shape) for kind in range(2)]
        for p in range(1, phases):
            hit = here == (1 << p)
            own = [jnp.where(hit, values[kind, p, p], own[kind]) for kind in range(2)]
        above_y = jnp.where(iota_y == ny - 1, here, shifted(here, 0, -1))
        above_z = jnp.where(iota_z == nz - 1, here, shifted(here, 1, -1))
        upper_y = faces(here, above_y)
        upper_z = faces(here, above_z)
        gaps, sums = ([], [])
        for kind in range(2):
            face[kind, 0, row] = jnp.where(iota_y == ny - 1, 0.0, upper_y[kind])
            face[kind, 1, row] = jnp.where(iota_z == nz - 1, 0.0, upper_z[kind])
            lower_y = jnp.where(iota_y == 0, own[kind], shifted(upper_y[kind], 0, 1))
            lower_z = jnp.where(iota_z == 0, own[kind], shifted(upper_z[kind], 1, 1))
            upper_x, lower_x = (self_x[kind, row], self_x[kind, row - 1])
            gaps.append([upper_x - lower_x, upper_y[kind] - lower_y, upper_z[kind] - lower_z])
            sums.append([upper_x + lower_x, upper_y[kind] + lower_y, upper_z[kind] + lower_z])
        global_row = first_row + row - halo
        inside = jnp.where((global_row >= 0) & (global_row < grid_rows), 1.0, 0.0)
        for c in range(3):
            kinds = [1 if a == c else 0 for a in range(3)]
            forcing = sum(strain[c][a] * gaps[kinds[a]][a] for a in range(3))
            diagonal = sums[kinds[0]][0] + sums[kinds[1]][1] + sums[kinds[2]][2]
            inverse = inside / diagonal
            rdiag[c, row] = inverse
            force[c, row] = forcing
            even[c, row] = forcing * inverse
        return carry

    lax.fori_loop(1, total - 1, setup, 0, unroll=7)

    buffers = (even, odd)
    for step in range(1, SWEEPS):
        source, target = (buffers[(step - 1) % 2], buffers[step % 2])

        def sweep(row, carry, source=source, target=target, last=step == SWEEPS - 1):
            for c in range(3):
                kx, ky, kz = (1 if a == c else 0 for a in range(3))
                here = source[c, row]
                face_y = face[ky, 0, row]
                face_z = face[kz, 1, row]
                summed = (
                    force[c, row]
                    + self_x[kx, row] * source[c, row + 1]
                    + self_x[kx, row - 1] * source[c, row - 1]
                    + face_y * shifted(here, 0, -1)
                    + shifted(face_y * here, 0, 1)
                    + face_z * shifted(here, 1, -1)
                    + shifted(face_z * here, 1, 1)
                )
                value = summed * rdiag[c, row]
                target[c, row] = value
                if last:
                    displace_ref[c, row - halo] = value
            return carry

        lax.fori_loop(1 + step, total - 1 - step, sweep, 0, unroll=4)

    band_rows = ny // bands
    for k in range(bands):
        band = me ^ k
        at = 0
        for b in range(band_rows // patch_y):
            start = pl.multiple_of(band * band_rows + b * patch_y, patch_y)
            for c in range(3):
                for x in range(0, slab, 2):
                    pair = jnp.concatenate(
                        [displace_ref[c, x + i, pl.ds(start, patch_y), :] for i in range(2)], axis=0
                    )
                    block_refs[k][pl.ds(at, 2 * patch_y), :] = pair.astype(bf16)
                    at += 2 * patch_y


def solve(phase, before, after, scalars, tables, loading, bands):
    slab, ny, nz = phase.shape
    total = slab + 2 * SWEEPS
    rows = 3 * slab * ny // bands
    smem = pl.BlockSpec(memory_space=pltpu.SMEM)
    vmem = pl.BlockSpec(memory_space=pltpu.VMEM)
    plane = (ny, nz)
    return pl.pallas_call(
        partial(solver_kernel, slab=slab, bands=bands, patch_y=PATCH_Y),
        out_shape=[jax.ShapeDtypeStruct((3, slab) + plane, f32)]
        + [jax.ShapeDtypeStruct((rows, nz), bf16)] * bands,
        in_specs=[smem, smem, smem, vmem, vmem, vmem],
        out_specs=[vmem] * (1 + bands),
        scratch_shapes=[
            pltpu.VMEM((total,) + plane, jnp.int32),
            pltpu.VMEM((2, 2, total) + plane, f32),
            pltpu.VMEM((2, total) + plane, f32),
            pltpu.VMEM((3, total) + plane, f32),
            pltpu.VMEM((3, total) + plane, f32),
            pltpu.VMEM((3, total) + plane, f32),
            pltpu.VMEM((3, total) + plane, f32),
        ],
        compiler_params=pltpu.CompilerParams(vmem_limit_bytes=30 * MIB),
        cost_estimate=pl.CostEstimate(flops=40_000_000, bytes_accessed=4_000_000, transcendentals=0),
        name="solver",
    )(scalars, tables, loading, phase, before, after)


def feature_order(features):
    feature = jnp.arange(features, dtype=jnp.int32)
    source = (feature % PATCH_Z) * (features // PATCH_Z) + feature // PATCH_Z
    return (feature[:, None] == source[None]).astype(bf16)


def patch_kernel(scalars, *refs, slabs, bands_in):
    block_refs, (perm_ref, order_ref, out_ref, plain_ref, held) = (refs[:slabs], refs[slabs:])
    rows, lanes = block_refs[0].shape
    rows = rows // bands_in
    me = scalars[0]
    for k in range(slabs):
        held[k] = block_refs[k][...]
    group = PATCH_Z
    for g in range(slabs * bands_in // group):
        parts = []
        for j in range(group):
            b, px = divmod(group * g + j, slabs)
            parts.append(held[me ^ px, pl.ds(b * rows, rows), :])
        moved = jnp.dot(
            jnp.concatenate(parts, axis=1), perm_ref[...], preferred_element_type=f32
        ).astype(bf16)
        for z in range(group):
            out_ref[pl.ds(z * rows, rows), pl.ds(g * lanes, lanes)] = moved[:, z * lanes : (z + 1) * lanes]
    plain_ref[...] = jnp.dot(order_ref[...], out_ref[...], preferred_element_type=f32).astype(bf16)


def patchify(blocks, scalars, bands_in):
    slabs = len(blocks)
    rows, nz = blocks[0].shape
    rows = rows // bands_in
    cells = nz // PATCH_Z
    width = PATCH_Z * nz
    features = PATCH_Z * rows
    tokens = slabs * bands_in * cells
    lane = jnp.arange(width, dtype=jnp.int32)
    j, pz, z = (lane // nz, lane % nz // PATCH_Z, lane % PATCH_Z)
    perm = ((z * nz + j * cells + pz)[:, None] == lane[None]).astype(bf16)
    order = feature_order(features).T
    vmem = pl.BlockSpec(memory_space=pltpu.VMEM)
    return pl.pallas_call(
        partial(patch_kernel, slabs=slabs, bands_in=bands_in),
        out_shape=[jax.ShapeDtypeStruct((features, tokens), bf16)] * 2,
        in_specs=[pl.BlockSpec(memory_space=pltpu.SMEM)] + [vmem] * (slabs + 2),
        out_specs=[vmem] * 2,
        scratch_shapes=[pltpu.VMEM((slabs, rows * bands_in, nz), bf16)],
        compiler_params=pltpu.CompilerParams(vmem_limit_bytes=12 * MIB),
        cost_estimate=pl.CostEstimate(flops=1_000_000_000, bytes_accessed=5_000_000, transcendentals=0),
        name="patchify",
    )(scalars, *blocks, perm, order)


def turn_kernel(scalars, cot_ref, own_ref, other_ref, held):
    per, hidden = own_ref.shape[:2]
    held[...] = cot_ref[...].T
    me, core = (scalars[0], scalars[1])
    for i in range(per):
        slot = (me % per) ^ i
        start = 2 * i * hidden
        own_ref[slot] = held[pl.ds(pl.multiple_of(start + core * hidden, hidden), hidden), :]
        other_ref[slot] = held[pl.ds(pl.multiple_of(start + (1 - core) * hidden, hidden), hidden), :]


def turn(cotangent, scalars, blocks, part):
    tokens, hidden = cotangent.shape
    width = hidden // blocks
    per = 1
    while per * width % 128:
        per *= 2
    steps = blocks // 2 // per
    out = jax.ShapeDtypeStruct((blocks // 2, width // 2, tokens), bf16)
    out_spec = pl.BlockSpec((per, width // 2, tokens), lambda i, s: (i, 0, 0))
    return pl.pallas_call(
        turn_kernel,
        out_shape=[out, out],
        grid_spec=pltpu.PrefetchScalarGridSpec(
            num_scalar_prefetch=1,
            grid=(steps,),
            in_specs=[
                pl.BlockSpec((tokens, per * width), lambda i, s: (0, (s[0] // per) ^ (part * steps + i)))
            ],
            out_specs=[out_spec, out_spec],
            scratch_shapes=[pltpu.VMEM((per * width, tokens), bf16)],
        ),
        compiler_params=pltpu.CompilerParams(vmem_limit_bytes=16 * MIB),
        cost_estimate=pl.CostEstimate(flops=0, bytes_accessed=3_200_000, transcendentals=0),
    )(scalars, cotangent)


def embed_kernel(w_ref, patch_ref, normed_ref, embed_ref, inverse_ref):
    model, tokens = embed_ref.shape
    tile = min(tokens, 256)
    for i in range(0, tokens, tile):
        cols = pl.ds(i, tile)
        value = jnp.dot(w_ref[...], patch_ref[:, cols], preferred_element_type=f32).astype(bf16)
        embed_ref[:, cols] = value
        wide = value.astype(f32)
        total = jnp.sum(wide * wide, axis=0, keepdims=True)
        inverse = lax.rsqrt(total / model + epsilon)
        inverse_ref[:, cols] = inverse
        normed_ref[:, cols] = (wide * inverse).astype(bf16)


def embed(w_all, patches):
    model, features = w_all.shape
    tokens = patches.shape[1]
    vmem = pl.BlockSpec(memory_space=pltpu.VMEM)
    return pl.pallas_call(
        embed_kernel,
        out_shape=[
            jax.ShapeDtypeStruct((model, tokens), bf16),
            jax.ShapeDtypeStruct((model, tokens), bf16),
            jax.ShapeDtypeStruct((1, tokens), f32),
        ],
        in_specs=[vmem] * 2,
        out_specs=[vmem] * 3,
        compiler_params=pltpu.CompilerParams(vmem_limit_bytes=16 * MIB),
        cost_estimate=pl.CostEstimate(
            flops=2 * model * features * tokens, bytes_accessed=6_000_000, transcendentals=0
        ),
    )(w_all, patches)


def join_kernel(scalars, even, odd, even_far, odd_far, order_ref, out_ref, held):
    half, rows = even.shape[:2]
    me, core = (scalars[0], scalars[1])
    for k in range(2 * half):
        start = (me ^ k) * (2 * rows)
        for part, source in ((core, (even, odd)), (1 - core, (even_far, odd_far))):
            at = pl.multiple_of(start + part * rows, 8)
            held[pl.ds(at, rows), :] = source[k & 1][k // 2].astype(f32)
    out_ref[...] = jnp.dot(held[...].astype(bf16), order_ref[...], preferred_element_type=f32).astype(bf16)


def join(parts, scalars):
    half, rows, features = parts[0].shape
    order = feature_order(features).T
    vmem = pl.BlockSpec(memory_space=pltpu.VMEM)
    return pl.pallas_call(
        join_kernel,
        out_shape=jax.ShapeDtypeStruct((4 * half * rows, features), bf16),
        in_specs=[pl.BlockSpec(memory_space=pltpu.SMEM)] + [vmem] * 5,
        out_specs=vmem,
        scratch_shapes=[pltpu.VMEM((4 * half * rows, features), f32)],
        compiler_params=pltpu.CompilerParams(vmem_limit_bytes=20 * MIB),
        cost_estimate=pl.CostEstimate(flops=1_700_000_000, bytes_accessed=5_000_000, transcendentals=0),
        name="join",
    )(scalars, *parts, order)


def tail_kernel(scalars, own_ref, far_ref, embed_ref, inverse_ref, plain_ref, *rest, slots):
    mine, (theirs, total, held) = (rest[:slots], rest[slots:])
    model = own_ref.shape[0]
    rows = model // (2 * slots)
    me, core = (scalars[0], scalars[1])
    inverse = inverse_ref[...]
    summed = own_ref[...] + far_ref[...].astype(f32)
    wide = embed_ref[...].astype(f32) * inverse
    inner = jnp.sum(summed * wide, axis=0, keepdims=True) / model
    total[...] = inverse * (summed - wide * inner)
    for k in range(slots):
        start = (me ^ k) * (2 * rows)
        for part in range(2):
            source = start + (core if part == 0 else 1 - core) * rows
            held[pl.ds((part * slots + k) * rows, rows), :] = total[pl.ds(pl.multiple_of(source, 8), rows), :]
    for part in (1, 0):
        grad = contract(
            held[pl.ds(part * slots * rows, slots * rows), :].astype(bf16), plain_ref[...], 1, 1
        ).astype(bf16)
        if part:
            theirs[...] = grad
        else:
            for k in range(slots):
                mine[k][...] = grad[k * rows : (k + 1) * rows]


def tail(own_grad, far_grad, embedded, inverse, plain, scalars, slots):
    model, tokens = own_grad.shape
    features = plain.shape[0]
    rows = model // (2 * slots)
    vmem = pl.BlockSpec(memory_space=pltpu.VMEM)
    return pl.pallas_call(
        partial(tail_kernel, slots=slots),
        out_shape=[jax.ShapeDtypeStruct((rows, features), bf16)] * slots
        + [jax.ShapeDtypeStruct((slots * rows, features), bf16)],
        in_specs=[pl.BlockSpec(memory_space=pltpu.SMEM)] + [vmem] * 5,
        out_specs=[vmem] * (slots + 1),
        scratch_shapes=[pltpu.VMEM((model, tokens), f32)] * 2,
        compiler_params=pltpu.CompilerParams(vmem_limit_bytes=28 * MIB),
        cost_estimate=pl.CostEstimate(flops=1_200_000_000, bytes_accessed=9_000_000, transcendentals=0),
        name="tail",
    )(scalars, own_grad, far_grad, embedded, inverse, plain)


def gelu_slope(value):
    scale = math.sqrt(2.0 / math.pi)
    square = value * value
    bend = jnp.tanh(value * (scale + (scale * 0.044715) * square))
    return 0.5 * (1.0 + bend) + 0.5 * value * (1.0 - bend * bend) * (
        scale + (3.0 * scale * 0.044715) * square
    )


def mlp_kernel(scalars, *refs, picks, count):
    held = sum(picks)
    w_refs, (normed_own, normed_far, cot_own, cot_far), outs = (
        list(refs[:held]),
        refs[held : held + 4],
        refs[held + 4 :],
    )
    act_own, act_far, w_out = outs[:3]
    grads = outs[3:]
    model, tokens = normed_own.shape
    hidden = w_out.shape[0] // count
    for k in range(count):
        if picks[k] == 1:
            w_out[pl.ds(k * hidden, hidden), :] = w_refs.pop(0)[...]
            continue
        mid = hidden // 2
        for half in (scalars[3], 1 - scalars[3]):
            at = pl.multiple_of(k * hidden + half * mid, mid)
            w_out[pl.ds(at, mid), :] = w_refs.pop(0)[...]
    tile = min(tokens, 256)
    for normed, cot, act in ((normed_own, cot_own, act_own), (normed_far, cot_far, act_far)):
        for i in range(0, tokens, tile):
            cols = pl.ds(i, tile)
            pre_act = jnp.dot(w_out[...], normed[:, cols], preferred_element_type=f32)
            cots = jnp.concatenate([cot[k, :, cols] for k in range(count)], axis=0).astype(f32)
            act[:, cols] = (cots * gelu_slope(pre_act)).astype(bf16)
    for i in range(0, model, 256):
        cols = pl.ds(i, min(256, model - i))
        value = contract(act_own[...], normed_own[cols, :], 1, 1)
        value = (value + contract(act_far[...], normed_far[cols, :], 1, 1)).astype(bf16)
        rows = grads[0].shape[0]
        for k in range(len(grads)):
            grads[k][:, cols] = value[k * rows : (k + 1) * rows]


def mlp(scalars, w_slots, normed, cots, pieces):
    count = len(w_slots)
    picks = tuple(len(pieces) for pieces in w_slots)
    w_pieces = [piece for pieces in w_slots for piece in pieces]
    hidden, model = w_slots[0][0].shape
    tokens = normed[0].shape[1]
    vmem = pl.BlockSpec(memory_space=pltpu.VMEM)
    cot_spec = pl.BlockSpec((count, hidden, tokens), lambda i: (0, 0, 0))
    whole = pl.BlockSpec((model, tokens), lambda i: (0, 0))
    slot = pl.BlockSpec((hidden // pieces, model), lambda i: (0, 0))
    wide = pl.BlockSpec((count * hidden, tokens), lambda i: (0, 0))
    return pl.pallas_call(
        partial(mlp_kernel, picks=picks, count=count),
        grid=(1,),
        out_shape=[jax.ShapeDtypeStruct((count * hidden, tokens), bf16)] * 2
        + [jax.ShapeDtypeStruct((count * hidden, model), bf16)]
        + [jax.ShapeDtypeStruct((hidden // pieces, model), bf16)] * (count * pieces),
        in_specs=[pl.BlockSpec(memory_space=pltpu.SMEM)]
        + [pl.BlockSpec(piece.shape, lambda i: (0, 0)) for piece in w_pieces]
        + [whole] * 2
        + [cot_spec] * 2,
        out_specs=[wide] * 2 + [pl.BlockSpec((count * hidden, model), lambda i: (0, 0))] + [slot] * (count * pieces),
        compiler_params=pltpu.CompilerParams(vmem_limit_bytes=30 * MIB),
        cost_estimate=pl.CostEstimate(
            flops=8 * count * hidden * model * tokens, bytes_accessed=15_000_000, transcendentals=0
        ),
    )(scalars, *w_pieces, *normed, *cots)


def bits_of(size):
    return [1 << i for i in range(size.bit_length() - 1)]


def gather_slots(slots, axis, order):
    for bit in order:
        for k in list(slots):
            slots[k ^ bit] = exchange(slots[k], axis, bit)
    return [slots[k] for k in sorted(slots)]


def reduce_slots(live, axis, order):
    live = dict(live)
    for bit in order:
        for k in sorted(k for k in live if k & bit):
            arrived = exchange(live.pop(k), axis, bit)
            live[k ^ bit] = (live[k ^ bit].astype(f32) + arrived.astype(f32)).astype(bf16)
    (last,) = live.values()
    return last


def scatter_slots(slots, axis, bits):
    half = len(slots) // 2
    turned = bits[1::-1] + bits[2:-1] if len(slots[half]) > 1 else bits[:-1]
    near = reduce_slots({k: slots[k] for k in range(half)}, axis, turned)
    pieces = len(slots[half])
    sums = []
    for i in range(pieces):
        far = reduce_slots({k: slots[k][i] for k in range(half, 2 * half)}, axis, bits[:-1])
        arrived = exchange(far, axis, half)
        rows = far.shape[0]
        sums.append(near[i * rows : (i + 1) * rows].astype(f32) + arrived.astype(f32))
    return jnp.concatenate(sums, axis=0) if pieces > 1 else sums[0]


def swap(value):
    return exchange(value, "rve", 1)


def local(phase, load_case, moduli, loading_table, w_embed, w_up, cotangent):
    phase = phase[0]
    slab, ny, _ = phase.shape
    devs = lax.axis_size("dev")
    bits = bits_of(devs)
    me = lax.axis_index("dev")
    core = lax.axis_index("rve")
    parity = lax.axis_index("groups") % 2
    features = w_embed.shape[1]
    rows_embed = w_embed.shape[0]
    hidden = w_up.shape[0]
    tokens = cotangent.shape[0]
    bands_in = ny // devs // PATCH_Y
    grad_scale = 1.0 / math.sqrt(tokens * devs * 2)

    small = phase.astype(bf16)
    up = [(i, i + 1) for i in range(devs - 1)]
    down = [(j, i) for i, j in up]
    before = lax.ppermute(small[slab - SWEEPS :], "dev", up)
    after = lax.ppermute(small[:SWEEPS], "dev", down)

    scalars = jnp.stack([me, core, load_case[0], parity]).astype(jnp.int32)
    outs = solve(phase, before, after, scalars, moduli, loading_table, devs)
    displace, blocks = (outs[0], outs[1:])

    near = [w_embed] + [exchange(w_embed, "dev", k) for k in range(2, devs, 2)]
    even = jnp.stack(near)
    odd = exchange(even, "dev", 1)
    w_all = join((even, odd, swap(even), swap(odd)), scalars)

    mid = hidden // 2

    def mine(value):
        return lax.dynamic_slice_in_dim(value, parity * mid, mid, 0)

    near = exchange(mine(w_up), "dev", devs // 2)
    far = exchange(near, "groups", 1)
    top = jnp.concatenate(
        [jnp.where(parity == 0, near, far), jnp.where(parity == 0, far, near)], axis=0
    )
    up_even = gather_slots({0: w_up, devs // 2: top}, "dev", bits[-2:0:-1])
    up_slots = []
    for i, value in enumerate(up_even):
        k = 2 * i + 1
        if k in (1, devs - 1):
            up_slots += [(value,), (exchange(value, "dev", 1),)]
        else:
            rows = mine(value)
            near = exchange(rows, "dev", 1)
            up_slots += [(value,), (near, exchange(near, "groups", 1))]

    cots = []
    for part in range(2):
        cot_own, cot_other = turn(cotangent, scalars, devs, part)
        cots.append((cot_own, swap(cot_other)))

    arrived = [blocks[0]] + [exchange(blocks[k], "dev", k) for k in range(1, devs)]
    patches, plain = patchify(arrived, scalars, bands_in)
    far_patches = swap(patches)
    normed_own, embedded, inverse_rms = embed(w_all, patches)
    normed_far, _, _ = embed(w_all, far_patches)

    half = devs // 2
    grads = []
    own_parts, far_parts, w_parts = ([], [], [])
    for part in range(2):
        act_own, act_far, w_part, *outs = mlp(
            scalars, up_slots[part * half : (part + 1) * half], (normed_own, normed_far), cots[part], 1 + part
        )
        grads += [tuple(outs[2 * k : 2 * k + 2]) for k in range(half)] if part else outs
        own_parts.append(act_own)
        far_parts.append(act_far)
        w_parts.append(w_part)
    grad_up = scatter_slots(grads, "dev", bits) * grad_scale

    far_grad = sum(contract(w, act, 0, 0) for w, act in zip(w_parts, far_parts)).astype(bf16)
    partner = swap(far_grad)
    own_grad = sum(contract(w, act, 0, 0) for w, act in zip(w_parts, own_parts))
    *mine, yours = tail(own_grad, partner, embedded, inverse_rms, plain, scalars, devs)
    arrived = swap(yours).reshape(devs, rows_embed, features)
    mine = [(m.astype(f32) + arrived[k].astype(f32)).astype(bf16) for k, m in enumerate(mine)]
    grad_embed = scatter_slots(mine[:half] + [(m,) for m in mine[half:]], "dev", bits) * grad_scale
    return (displace[None], grad_embed, grad_up)


def solution(mesh):
    return jax.shard_map(
        local,
        mesh=mesh,
        in_specs=(
            P(("groups", "rve"), "dev", None, None),
            P(("groups", "rve")),
            P(),
            P(),
            P(("dev", "rve"), None),
            P(("dev", "rve"), None),
            P(("groups", "dev", "rve"), None),
        ),
        out_specs=(
            P(("groups", "rve"), None, "dev", None, None),
            P(("groups", "dev", "rve"), None),
            P(("groups", "dev", "rve"), None),
        ),
        check_vma=False,
    )
```
